256 devices in a mesh: lon: 8 (over z), lat: 8 (over x, y_hi), dp: 4 (over y_lo, core).
Axes of the slice: x: 4, y: 4 (y_hi: 2, y_lo: 2; y = y_hi * 2 + y_lo), z: 8, core: 2. Of those that a mesh axis runs over, the one named last changes fastest.
Arguments:
- fields: bfloat16 [4, 256, 64, 1024], P('dp', None, 'lat', 'lon'), may hold values from -6 to 6
- weight_one: bfloat16 [9, 256, 256], replicated, may hold values from -0.125 to 0.125
- weight_two: bfloat16 [9, 256, 256], replicated, may hold values from -0.125 to 0.125
- edge_flips: int32 [7, 8], replicated, may hold values from 0 to 1, as said below
- cotangent: bfloat16 [4, 256, 64, 1024], P('dp', None, 'lat', 'lon'), may hold values from -6 to 6
Outputs:
- output: bfloat16 [4, 256, 64, 1024], P('dp', None, 'lat', 'lon')
- grad_fields: bfloat16 [4, 256, 64, 1024], P('dp', None, 'lat', 'lon')
- grad_one: float32 [9, 256, 256], replicated
- grad_two: float32 [9, 256, 256], replicated
The draws below stay inside these ranges and needn't reach their ends.
Inputs may be any that keep to these rules, and one draw needn't show every extreme that they name: `edge_flips`: 0 on every edge inside a face; only row 8 // 2 - 1, the boundary between the band's two face rows, may hold 1, where the two faces meeting at that longitude tile store longitude in opposite orders.
All inputs are finite; a program needn't handle non-finite values.
Results may differ from the reference program's by a relative error of at most 0.0034.
Values may be sent and summed in bfloat16 or wider, within the bound.
No kernel may reach another device: no remote copies, remote signals or barrier semaphores. Data moves between devices by JAX's collectives and lax.ppermute only.
A program may use at most 128 MiB of HBM per device.

```python
import jax
import jax.numpy as jnp

CH = 256
ROWS = 8
COLS = 128
BATCH = 4
LAT_CELLS = 64
LON_CELLS = 1024
N_LON = 8
N_LAT = 8


def draw_edge_flips(key, part):
    first_key = jax.random.fold_in(key, 11)
    second_key = jax.random.fold_in(key, 12)
    random_bits = jax.random.randint(first_key, (N_LON,), 0, 2).astype(jnp.int32)
    chosen = jax.random.randint(second_key, (), 0, N_LON).astype(jnp.int32)
    columns = jnp.arange(N_LON, dtype=jnp.int32)
    line_flags = jnp.where(columns == chosen, 1, jnp.where(columns == (chosen + 1) % N_LON, 0, random_bits)).astype(jnp.int32)
    edge_rows = jnp.arange(N_LAT - 1, dtype=jnp.int32)[:, None]
    boundary = N_LAT // 2 - 1
    return jnp.where(edge_rows == boundary, line_flags[None, :], 0).astype(jnp.int32)


def shard_levels(own_key, shape, pieces, smallest, top_value):
    def one(position, blocks):
        steps = jax.random.uniform(jax.random.fold_in(jax.random.fold_in(own_key, 6), position), (blocks,), jnp.float32, smallest / len(pieces), top_value / len(pieces))
        return jnp.repeat(jnp.exp(steps), shape[position] // blocks).reshape((-1,) + (1,) * (len(shape) - position - 1))

    level = one(*pieces[0])
    for cut in pieces[1:]:
        level = level * one(*cut)
    return level


def centred(rng, shape, scale, reach, shards=(), kind=jnp.bfloat16):
    entries = jax.random.normal(rng, shape, jnp.float32) * scale
    if len(shards) > 0:
        entries = shard_levels(rng, shape, shards, -0.22, 0.18) * entries
    return jnp.clip(entries, min=-reach, max=reach).astype(kind)


def setup_inputs(seed: int = 0) -> dict:
    seeds = jax.random.split(jax.random.key(seed), 6)
    return {
        "fields": centred(seeds[0], (BATCH, CH, LAT_CELLS, LON_CELLS), 1.0, 6.0, ((0, 4), (2, 8), (3, 8))),
        "weight_one": centred(seeds[1], (9, CH, CH), (9 * CH) ** -0.5, 0.125),
        "weight_two": centred(seeds[2], (9, CH, CH), (9 * CH) ** -0.5, 0.125),
        "edge_flips": draw_edge_flips(jax.random.fold_in(seeds[5], 71), 0),
        "cotangent": centred(seeds[4], (BATCH, CH, LAT_CELLS, LON_CELLS), 1.0, 6.0, ((0, 4), (2, 8), (3, 8))),
    }


def tiles_of(source):
    batch, chans = (source.shape[0], source.shape[1])
    shaped = source.reshape(batch, chans, N_LAT, ROWS, N_LON, COLS)
    return jnp.transpose(shaped, (2, 4, 0, 1, 3, 5))

def field_of(tiles):
    batch, chans = (tiles.shape[2], tiles.shape[3])
    shaped = jnp.transpose(tiles, (2, 3, 0, 4, 1, 5))
    return shaped.reshape(batch, chans, N_LAT * ROWS, N_LON * COLS)

def pad_tiles(tiles, edge_flips):
    west = jnp.roll(tiles[..., -1:], 1, axis=1)
    east = jnp.roll(tiles[..., :1], -1, axis=1)
    extended = jnp.concatenate([west, tiles, east], -1)
    reverse = edge_flips[:, :, None, None, None]
    north_src = extended[:-1, :, :, :, -1, :]
    top_rim = jnp.where(reverse == 1, jnp.flip(north_src, -1), north_src)
    top_rim = jnp.concatenate([jnp.zeros_like(top_rim[:1]), top_rim], 0)
    south_src = extended[1:, :, :, :, 0, :]
    bottom = jnp.where(reverse == 1, jnp.flip(south_src, -1), south_src)
    bottom = jnp.concatenate([bottom, jnp.zeros_like(bottom[:1])], 0)
    return jnp.concatenate([top_rim[..., None, :], extended, bottom[..., None, :]], -2)

def convolve(padded_in, weight):
    total = None
    for tap_row in range(3):
        for tap_col in range(3):
            piece = padded_in[..., tap_row:tap_row + ROWS, tap_col:tap_col + COLS].astype(jnp.float32)
            term = jnp.einsum('oc,anbchw->anbohw', weight[3 * tap_row + tap_col].astype(jnp.float32), piece)
            total = term if total is None else total + term
    return total

def transposed(grad_tiles, weight):
    shape = grad_tiles.shape[:-2] + (ROWS + 2, COLS + 2)
    padded_grad = jnp.zeros(shape, jnp.float32)
    for tap_row in range(3):
        for tap_col in range(3):
            term = jnp.einsum('oc,anbohw->anbchw', weight[3 * tap_row + tap_col].astype(jnp.float32), grad_tiles.astype(jnp.float32))
            padded_grad = padded_grad.at[..., tap_row:tap_row + ROWS, tap_col:tap_col + COLS].add(term)
    return padded_grad

def kernel_grad(grad_tiles, padded_in):
    taps = []
    for tap_row in range(3):
        for tap_col in range(3):
            piece = padded_in[..., tap_row:tap_row + ROWS, tap_col:tap_col + COLS].astype(jnp.float32)
            taps.append(jnp.einsum('anbohw,anbchw->oc', grad_tiles.astype(jnp.float32), piece))
    return jnp.stack(taps, 0)

def reference(fields, weight_one, weight_two, edge_flips, cotangent):
    tile_view = tiles_of(fields)
    padded_in = pad_tiles(tile_view, edge_flips)
    hidden = convolve(padded_in, weight_one)
    activation = jax.nn.silu(hidden).astype(jnp.bfloat16)
    padded_act = pad_tiles(activation, edge_flips)
    output = (tile_view.astype(jnp.float32) + convolve(padded_act, weight_two)).astype(jnp.bfloat16)
    cot_tiles = tiles_of(cotangent)
    grad_two = kernel_grad(cot_tiles, padded_act)
    _, pullback = jax.vjp(lambda source: pad_tiles(source, edge_flips), jnp.zeros(tile_view.shape, jnp.float32))
    back_act = pullback(transposed(cot_tiles, weight_two))[0]
    sigmoid_h = jax.nn.sigmoid(hidden)
    back_hidden = (back_act * sigmoid_h * (1.0 + hidden * (1.0 - sigmoid_h))).astype(jnp.bfloat16)
    grad_one = kernel_grad(back_hidden, padded_in)
    grad_tiles = cot_tiles.astype(jnp.float32) + pullback(transposed(back_hidden, weight_one))[0]
    return (field_of(output), field_of(grad_tiles.astype(jnp.bfloat16)), grad_one, grad_two)
```

```python
import jax
import jax.numpy as jnp
from jax import lax
from jax.experimental import pallas as pl
from jax.experimental.pallas import tpu as pltpu
from jax.sharding import PartitionSpec as P

F32 = jnp.float32
BF16 = jnp.bfloat16
LANES = 128
ROWS = 8
CELLS = ROWS * LANES
PADDED = CELLS + 2 * LANES
NT = (((1,), (1,)), ((), ()))
TN = (((0,), (0,)), ((), ()))


def iota(shape, dim):
    return lax.broadcasted_iota(jnp.int32, shape, dim)


def one_hot(cond):
    return jnp.where(cond, 1.0, 0.0).astype(BF16)


def dot(a, b):
    return jnp.dot(a, b, preferred_element_type=F32)


def rims(first, second, flags, outs):
    east, west, south, north, se, sw, ne, nw = outs
    shape = (2 * ROWS, CELLS)
    row, cell = (iota(shape, 0), iota(shape, 1))
    pick = one_hot(cell == jnp.where(row < ROWS, row * LANES + LANES - 1, (row - ROWS) * LANES))
    one = lax.dot_general(pick, first, NT, preferred_element_type=F32)
    two = lax.dot_general(pick, second, NT, preferred_element_type=F32)
    east[...] = jnp.concatenate([one[:ROWS], two[:ROWS]], 0).astype(BF16)
    west[...] = jnp.concatenate([one[ROWS:], two[ROWS:]], 0).astype(BF16)
    chans = first.shape[0]
    south[:chans] = first[:, CELLS - LANES :]
    south[chans:] = second[:, CELLS - LANES :]
    north[:chans] = first[:, :LANES]
    north[chans:] = second[:, :LANES]
    upper, lower = (flags[0] == 1, flags[1] == 1)
    top, last = (0, ROWS - 1)

    def corner(out, mine, other, flip):
        pair = jnp.where(flip, two[other : other + 1], two[mine : mine + 1])
        head = jnp.broadcast_to(one[mine : mine + 1], (ROWS, chans))
        tail = jnp.broadcast_to(pair, (ROWS, chans))
        out[...] = jnp.where(iota((ROWS, chans), 0) == 0, head, tail).astype(BF16)

    corner(se, last, last + ROWS, lower)
    corner(sw, last + ROWS, last, lower)
    corner(ne, top, top + ROWS, upper)
    corner(nw, top + ROWS, top, upper)


def turned(line, flip):
    shape = (LANES, LANES)
    a, b = (iota(shape, 0), iota(shape, 1))
    turn = one_hot(b == a + flip * (LANES - 1 - 2 * a))
    return dot(line, turn)


def shifted(out, centre, top, bottom, west, east, swap_top=None, swap_bottom=None):
    chans = centre.shape[0]
    k, lane = (iota((16, PADDED), 0), iota((16, PADDED), 1))
    placed_west = lax.dot_general(
        west, one_hot(lane == k * LANES), TN, preferred_element_type=F32
    )
    placed_east = lax.dot_general(
        east, one_hot(lane == k * LANES + LANES - 1), TN, preferred_element_type=F32
    )
    lane_in = iota((chans, LANES), 1)
    for block in range(ROWS + 2):
        span = slice(block * LANES, (block + 1) * LANES)
        if block == 0:
            line = top
        elif block == ROWS + 1:
            line = bottom
        else:
            line = centre[:, (block - 1) * LANES : block * LANES].astype(F32)
        left = jnp.where(lane_in == 0, placed_west[:, span], pltpu.roll(line, 1, 1))
        right = jnp.where(lane_in == LANES - 1, placed_east[:, span], pltpu.roll(line, LANES - 1, 1))
        swap = swap_top if block == 0 else swap_bottom if block == ROWS + 1 else None
        if swap is not None:
            left, right = (jnp.where(swap, right, left), jnp.where(swap, left, right))
        out[0, :, span] = left.astype(BF16)
        out[1, :, span] = line.astype(BF16)
        out[2, :, span] = right.astype(BF16)


def lines(top, mid, bottom):
    return jnp.concatenate([top, mid, bottom, jnp.zeros((6, mid.shape[1]), F32)], 0).astype(BF16)


def pad_forward(out, centre, flags, halo):
    from_w, from_e, from_n, from_s, c_nw, c_ne, c_sw, c_se = halo
    chans = centre.shape[0]
    upper, lower = (flags[0] == 1, flags[1] == 1)
    get = lambda ref: ref[...].astype(F32)[:1]
    nw, ne, sw, se = (get(c_nw), get(c_ne), get(c_sw), get(c_se))
    west = lines(jnp.where(upper, ne, nw), from_w[...].astype(F32)[:ROWS], jnp.where(lower, se, sw))
    east = lines(jnp.where(upper, nw, ne), from_e[...].astype(F32)[:ROWS], jnp.where(lower, sw, se))
    top = turned(from_n[:chans], flags[0])
    bottom = turned(from_s[:chans], flags[1])
    shifted(out, centre, top, bottom, west, east)


def pad_backward(out, centre, flags, halo):
    from_w, from_e, from_n, from_s = halo[:4]
    chans = centre.shape[0]
    upper, lower = (flags[0] == 1, flags[1] == 1)
    none = jnp.zeros((1, chans), F32)
    west = lines(none, from_w[...].astype(F32)[ROWS:], none)
    east = lines(none, from_e[...].astype(F32)[ROWS:], none)
    top = turned(from_n[chans:], flags[0])
    bottom = turned(from_s[chans:], flags[1])
    shifted(out, centre, top, bottom, west, east, upper, lower)


def conv(weight, pads):
    total = None
    for tap in range(9):
        r, s = divmod(tap, 3)
        term = dot(weight[tap], pads[s, :, r * LANES : r * LANES + CELLS])
        total = term if total is None else total + term
    return total


def conv_adjoint(weight, pads, flags, halo):
    total = None
    for tap in range(9):
        r, s = divmod(tap, 3)
        start = (2 - r) * LANES
        term = lax.dot_general(
            weight[tap], pads[2 - s, :, start : start + CELLS], TN, preferred_element_type=F32
        )
        total = term if total is None else total + term
    c_nw, c_ne, c_sw, c_se = halo[4:]
    chans = total.shape[0]
    k, lane = (iota((ROWS, LANES), 0), iota((ROWS, LANES), 1))

    def corner(ref, at, tap):
        spread = lax.dot_general(
            ref[...], one_hot((k == 1) & (lane == at)), TN, preferred_element_type=F32
        ).astype(BF16)
        return lax.dot_general(weight[tap], spread, TN, preferred_element_type=F32)

    top = corner(c_nw, 0, 8 - 2 * flags[2]) + corner(c_ne, LANES - 1, 6 + 2 * flags[3])
    bottom = corner(c_sw, 0, 2 - 2 * flags[4]) + corner(c_se, LANES - 1, 2 * flags[5])
    return jnp.concatenate(
        [total[:, :LANES] + top, total[:, LANES : CELLS - LANES], total[:, CELLS - LANES :] + bottom],
        1,
    )


def prepare_kernel(flags, first, second, *outs):
    rims(first[...], second[...], flags, outs)


def hidden_kernel(flags, field, cotangent, one, two, *refs):
    halo, outs, back_pads = (refs[:8], refs[8:-1], refs[-1])
    act_out, back_out, pads = outs[:3]
    pad_forward(pads, field[...], flags, halo)
    pad_backward(back_pads, cotangent[...], flags, halo)
    hidden = conv(one, pads)
    back_act = conv_adjoint(two, back_pads, flags, halo)
    sigma = 1.0 / (1.0 + jnp.exp(-hidden))
    act_out[...] = (hidden * sigma).astype(BF16)
    back_out[...] = (back_act * sigma * (1.0 + hidden * (1.0 - sigma))).astype(BF16)
    rims(act_out[...], back_out[...], flags, outs[3:])


def grad_kernel(grad_tile, pads, out):
    for tap in range(9):
        r, s = divmod(tap, 3)
        out[tap] = lax.dot_general(
            grad_tile[...], pads[s, :, r * LANES : r * LANES + CELLS], NT, preferred_element_type=F32
        )


def grad_two_kernel(flags, act, cotangent, *refs):
    halo, pads, out = (refs[:8], refs[8], refs[9])
    pad_forward(pads, act[...], flags, halo)
    grad_kernel(cotangent, pads, out)


def result_kernel(flags, field, cotangent, back, one, two, pads, *refs):
    halo, (output, grad_fields, back_pads) = (refs[:8], refs[8:])
    output[...] = (field[...].astype(F32) + conv(two, pads)).astype(BF16)
    pad_backward(back_pads, back[...], flags, halo)
    grad_fields[...] = (
        cotangent[...].astype(F32) + conv_adjoint(one, back_pads, flags, halo)
    ).astype(BF16)


SMEM = pl.BlockSpec(memory_space=pltpu.SMEM)
VMEM = pl.BlockSpec(memory_space=pltpu.VMEM)


def call(kernel, name, out_shape, args, scratch=(), flags=True):
    return pl.pallas_call(
        kernel,
        name=name,
        out_shape=out_shape,
        in_specs=([SMEM] if flags else []) + [VMEM] * (len(args) - (1 if flags else 0)),
        out_specs=jax.tree.map(lambda _: VMEM, out_shape),
        scratch_shapes=list(scratch),
        compiler_params=pltpu.CompilerParams(vmem_limit_bytes=56 * 1024 * 1024),
    )(*args)


def struct(*shape, dtype=BF16):
    return jax.ShapeDtypeStruct(shape, dtype)


def rim_shapes(chans):
    side = struct(2 * ROWS, chans)
    line = struct(2 * chans, LANES)
    corner = struct(ROWS, chans)
    return (side, side, line, line, corner, corner, corner, corner)


def exchange(rim):
    east, west, south, north, se, sw, ne, nw = rim
    lons, lats = (lax.axis_size("lon"), lax.axis_size("lat"))

    def along(value, step):
        return lax.ppermute(value, "lon", [(i, (i + step) % lons) for i in range(lons)])

    def across(value, step):
        return lax.ppermute(
            value, "lat", [(i, i + step) for i in range(lats) if 0 <= i + step < lats]
        )

    def diagonal(value, down, right):
        pairs = [
            (o * lats + a, ((o + right) % lons) * lats + a + down)
            for o in range(lons)
            for a in range(lats)
            if 0 <= a + down < lats
        ]
        return lax.ppermute(value, ("lon", "lat"), pairs)

    from_n, from_s = (across(south, 1), across(north, -1))
    c_nw, c_ne = (diagonal(se, 1, 1), diagonal(sw, 1, -1))
    c_sw, c_se = (diagonal(ne, -1, 1), diagonal(nw, -1, -1))
    from_w, from_e = (along(east, 1), along(west, -1))
    return (from_w, from_e, from_n, from_s, c_nw, c_ne, c_sw, c_se)


def edge_flags(edge_flips):
    a, o = (lax.axis_index("lat"), lax.axis_index("lon"))
    lats, lons = (lax.axis_size("lat"), lax.axis_size("lon"))
    rows = lax.dynamic_slice(
        jnp.concatenate([jnp.zeros((1, lons), jnp.int32), edge_flips, jnp.zeros((1, lons), jnp.int32)]),
        (a, 0),
        (2, lons),
    )
    wide = jnp.concatenate([rows[:, -1:], rows, rows[:, :1]], 1)
    near = lax.dynamic_slice(wide, (0, o), (2, 3))
    return jnp.stack(
        [near[0, 1], near[1, 1], near[0, 0], near[0, 2], near[1, 0], near[1, 2]]
    )


def sum_over(value, axis, dtype):
    count = lax.axis_size(axis)
    parts = value.reshape(count, value.shape[0] // count, value.shape[1]).astype(dtype)
    return jnp.sum(lax.all_to_all(parts, axis, 0, 0).astype(F32), 0)


def spread_over(value, axis):
    count = lax.axis_size(axis)
    same = jnp.broadcast_to(value[None], (count,) + value.shape)
    got = lax.all_to_all(same, axis, 0, 0)
    return got.reshape(count * value.shape[0], value.shape[1])


def reduce_grads(one, two):
    chans = one.shape[-1]
    one, two = (one.reshape(-1, chans), two.reshape(-1, chans))
    place = lax.axis_index("dp")
    core, side = (place % 2, place // 2)
    got_one = lax.ppermute(one.astype(BF16), "dp", [(1, 0), (3, 2)])
    got_two = lax.ppermute(two.astype(BF16), "dp", [(0, 1), (2, 3)])
    mine = jnp.where(core == 0, one + got_one.astype(F32), two + got_two.astype(F32))
    half = mine.shape[0] // 2
    away = lax.dynamic_slice_in_dim(mine, (1 - side) * half, half, 0).astype(BF16)
    kept = lax.dynamic_slice_in_dim(mine, side * half, half, 0)
    got = lax.ppermute(away, "dp", [(i, (i + 2) % 4) for i in range(4)])
    part = sum_over(kept + got.astype(F32), "lat", BF16)
    part = sum_over(part, "lon", F32).astype(BF16)
    part = spread_over(spread_over(part, "lon"), "lat")
    other = lax.ppermute(part, "dp", [(i, (i + 2) % 4) for i in range(4)])
    full = jnp.where(
        side == 0, jnp.concatenate([part, other], 0), jnp.concatenate([other, part], 0)
    )
    pair = lax.ppermute(full, "dp", [(0, 1), (1, 0), (2, 3), (3, 2)])
    out_one = jnp.where(core == 0, full, pair).astype(F32)
    out_two = jnp.where(core == 0, pair, full).astype(F32)
    return (out_one.reshape(9, chans, chans), out_two.reshape(9, chans, chans))


def per_device(fields, weight_one, weight_two, edge_flips, cotangent):
    chans = fields.shape[1]
    flat = (chans, CELLS)
    field, cot = (fields.reshape(flat), cotangent.reshape(flat))
    flags = edge_flags(edge_flips)
    pads = struct(3, chans, PADDED)
    scratch = [pltpu.VMEM((3, chans, PADDED), BF16)]
    rim = call(prepare_kernel, "prepare", rim_shapes(chans), (flags, field, cot))
    halo = exchange(rim)
    act, back, pads_in, *rim = call(
        hidden_kernel,
        "hidden",
        (struct(*flat), struct(*flat), pads) + rim_shapes(chans),
        (flags, field, cot, weight_one, weight_two) + halo,
        scratch,
    )
    halo = exchange(rim)
    local = struct(9, chans, chans, dtype=F32)
    local_one = call(grad_kernel, "grad_one", local, (back, pads_in), flags=False)
    pads_act, local_two = call(grad_two_kernel, "grad_two", (pads, local), (flags, act, cot) + halo)
    grad_one, grad_two = reduce_grads(local_one, local_two)
    output, grad_fields = call(
        result_kernel,
        "result",
        (struct(*flat), struct(*flat)),
        (flags, field, cot, back, weight_one, weight_two, pads_act) + halo,
        scratch,
    )
    return (output.reshape(fields.shape), grad_fields.reshape(fields.shape), grad_one, grad_two)


def solution(mesh):
    in_specs = (P("dp", None, "lat", "lon"), P(), P(), P(), P("dp", None, "lat", "lon"))
    out_specs = (P("dp", None, "lat", "lon"), P("dp", None, "lat", "lon"), P(), P())
    return jax.shard_map(
        per_device, mesh=mesh, in_specs=in_specs, out_specs=out_specs, check_vma=False
    )
```

```python
import jax
import jax.numpy as jnp
from jax import lax
from jax.experimental import pallas as pl
from jax.experimental.pallas import tpu as pltpu
from jax.sharding import PartitionSpec as P

F32 = jnp.float32
BF16 = jnp.bfloat16
LANES = 128
ROWS = 8
CELLS = ROWS * LANES
PADDED = CELLS + 2 * LANES
NT = (((1,), (1,)), ((), ()))
TN = (((0,), (0,)), ((), ()))


def iota(shape, dim):
    return lax.broadcasted_iota(jnp.int32, shape, dim)


def one_hot(cond):
    return jnp.where(cond, 1.0, 0.0).astype(BF16)


def dot(a, b):
    return jnp.dot(a, b, preferred_element_type=F32)


def edge_flags(flips):
    a, o = (lax.axis_index("lat"), lax.axis_index("lon"))
    edges, lons = flips.shape

    def upper(col):
        return jnp.where(a > 0, flips[jnp.maximum(a - 1, 0), col], 0)

    def lower(col):
        return jnp.where(a < edges, flips[jnp.minimum(a, edges - 1), col], 0)

    west, east = (lax.rem(o + lons - 1, lons), lax.rem(o + 1, lons))
    return (upper(o), lower(o), upper(west), upper(east), lower(west), lower(east))


def rims(first, second, flags, outs):
    east, west, south, north = outs
    shape = (2 * ROWS, CELLS)
    row, cell = (iota(shape, 0), iota(shape, 1))
    pick = one_hot(cell == jnp.where(row < ROWS, row * LANES + LANES - 1, (row - ROWS) * LANES))
    one = lax.dot_general(pick, first, NT, preferred_element_type=F32)
    two = lax.dot_general(pick, second, NT, preferred_element_type=F32)
    chans = first.shape[0]
    upper, lower = (flags[0] == 1, flags[1] == 1)
    end = ROWS - 1

    def side(out, base, far):
        top = jnp.where(upper, two[far : far + 1], two[base : base + 1])
        low = jnp.where(lower, two[far + end : far + ROWS], two[base + end : base + ROWS])
        at = iota((ROWS, chans), 0)
        corners = jnp.where(at == 0, jnp.broadcast_to(top, at.shape), jnp.broadcast_to(low, at.shape))
        out[...] = jnp.concatenate(
            [one[base : base + ROWS], two[base : base + ROWS], corners, corners], 0
        ).astype(BF16)

    side(east, 0, ROWS)
    side(west, ROWS, 0)
    south[:chans] = first[:, CELLS - LANES :]
    south[chans:] = second[:, CELLS - LANES :]
    north[:chans] = first[:, :LANES]
    north[chans:] = second[:, :LANES]


def join_kernel(south, north, from_w, from_e, south_out, north_out):
    rows = south.shape[0]
    west, east = (from_w[...].astype(F32), from_e[...].astype(F32))
    at = iota((16, west.shape[1]), 0)
    for rim, out, near, corner in ((south, south_out, 7, 17), (north, north_out, 0, 16)):
        out[:rows] = rim[...]
        spread = [
            jnp.broadcast_to(side[k : k + 1], at.shape)
            for side in (west, east)
            for k in (near, corner)
        ]
        block = jnp.where(
            at == 0, spread[0], jnp.where(at == 1, spread[1], jnp.where(at == 2, spread[2], spread[3]))
        ).astype(BF16)
        out[rows : rows + 16] = block[:, :LANES]
        out[rows + 16 :] = block[:, LANES:]


def corners_of(line, chans):
    rows = 2 * chans
    return jnp.concatenate([line[rows : rows + 16], line[rows + 16 : rows + 32]], 1)


def turned(line, flip):
    shape = (LANES, LANES)
    a, b = (iota(shape, 0), iota(shape, 1))
    turn = one_hot(b == a + flip * (LANES - 1 - 2 * a))
    return dot(line, turn)


def shifted(out, centre, top, bottom, west, east, swap_top=None, swap_bottom=None):
    chans = centre.shape[0]
    k, lane = (iota((16, PADDED), 0), iota((16, PADDED), 1))
    placed_west = lax.dot_general(
        west, one_hot(lane == k * LANES), TN, preferred_element_type=F32
    )
    placed_east = lax.dot_general(
        east, one_hot(lane == k * LANES + LANES - 1), TN, preferred_element_type=F32
    )
    lane_in = iota((chans, LANES), 1)
    for block in range(ROWS + 2):
        span = slice(block * LANES, (block + 1) * LANES)
        if block == 0:
            line = top
        elif block == ROWS + 1:
            line = bottom
        else:
            line = centre[:, (block - 1) * LANES : block * LANES].astype(F32)
        left = jnp.where(lane_in == 0, placed_west[:, span], pltpu.roll(line, 1, 1))
        right = jnp.where(lane_in == LANES - 1, placed_east[:, span], pltpu.roll(line, LANES - 1, 1))
        swap = swap_top if block == 0 else swap_bottom if block == ROWS + 1 else None
        if swap is not None:
            left, right = (jnp.where(swap, right, left), jnp.where(swap, left, right))
        out[0, :, span] = left.astype(BF16)
        out[1, :, span] = line.astype(BF16)
        out[2, :, span] = right.astype(BF16)


def lines(top, mid, bottom):
    return jnp.concatenate([top, mid, bottom, jnp.zeros((6, mid.shape[1]), F32)], 0).astype(BF16)


def pad_forward(out, centre, flags, halo):
    from_w, from_e, from_n, from_s = halo
    chans = centre.shape[0]
    upper, lower = (flags[0] == 1, flags[1] == 1)
    above, below = (corners_of(ref, chans).astype(F32) for ref in (from_n, from_s))
    nw, ne, sw, se = (above[:1], above[2:3], below[:1], below[2:3])
    west = lines(jnp.where(upper, ne, nw), from_w[...].astype(F32)[:ROWS], jnp.where(lower, se, sw))
    east = lines(jnp.where(upper, nw, ne), from_e[...].astype(F32)[:ROWS], jnp.where(lower, sw, se))
    top = turned(from_n[:chans], flags[0])
    bottom = turned(from_s[:chans], flags[1])
    shifted(out, centre, top, bottom, west, east)


def pad_backward(out, centre, flags, halo):
    from_w, from_e, from_n, from_s = halo
    chans = centre.shape[0]
    upper, lower = (flags[0] == 1, flags[1] == 1)
    none = jnp.zeros((1, chans), F32)
    west = lines(none, from_w[...].astype(F32)[ROWS : 2 * ROWS], none)
    east = lines(none, from_e[...].astype(F32)[ROWS : 2 * ROWS], none)
    top = turned(from_n[chans : 2 * chans], flags[0])
    bottom = turned(from_s[chans : 2 * chans], flags[1])
    shifted(out, centre, top, bottom, west, east, upper, lower)


def conv(weight, pads):
    total = None
    for tap in range(9):
        r, s = divmod(tap, 3)
        term = dot(weight[tap], pads[s, :, r * LANES : r * LANES + CELLS])
        total = term if total is None else total + term
    return total


def conv_adjoint(weight, pads, flags, halo):
    total = None
    for tap in range(9):
        r, s = divmod(tap, 3)
        start = (2 - r) * LANES
        term = lax.dot_general(
            weight[tap], pads[2 - s, :, start : start + CELLS], TN, preferred_element_type=F32
        )
        total = term if total is None else total + term
    chans = total.shape[0]
    above, below = (corners_of(ref, chans) for ref in halo[2:])
    k, lane = (iota((16, LANES), 0), iota((16, LANES), 1))

    def corner(block, which, at, tap):
        spread = lax.dot_general(
            block, one_hot((k == which) & (lane == at)), TN, preferred_element_type=F32
        ).astype(BF16)
        return lax.dot_general(weight[tap], spread, TN, preferred_element_type=F32)

    east = LANES - 1
    top = corner(above, 1, 0, 8 - 2 * flags[2]) + corner(above, 3, east, 6 + 2 * flags[3])
    bottom = corner(below, 1, 0, 2 - 2 * flags[4]) + corner(below, 3, east, 2 * flags[5])
    return jnp.concatenate(
        [total[:, :LANES] + top, total[:, LANES : CELLS - LANES], total[:, CELLS - LANES :] + bottom],
        1,
    )


def prepare_kernel(flips, field, cotangent, *outs):
    flat_field, flat_cot = outs[:2]
    for row in range(ROWS):
        span = slice(row * LANES, (row + 1) * LANES)
        flat_field[:, span] = field[:, row, :]
        flat_cot[:, span] = cotangent[:, row, :]
    rims(flat_field[...], flat_cot[...], edge_flags(flips), outs[2:])


def hidden_kernel(flips, field, cotangent, one, two, *refs):
    halo, outs, back_pads = (refs[:4], refs[4:-1], refs[-1])
    act_out, back_out, pads = outs[:3]
    flags = edge_flags(flips)
    pad_forward(pads, field[...], flags, halo)
    pad_backward(back_pads, cotangent[...], flags, halo)
    hidden = conv(one, pads)
    back_act = conv_adjoint(two, back_pads, flags, halo)
    sigma = 1.0 / (1.0 + jnp.exp(-hidden))
    act_out[...] = (hidden * sigma).astype(BF16)
    back_out[...] = (back_act * sigma * (1.0 + hidden * (1.0 - sigma))).astype(BF16)
    rims(act_out[...], back_out[...], flags, outs[3:])


def grad_kernel(grad_tile, pads, out, out_low):
    for tap in range(9):
        r, s = divmod(tap, 3)
        term = lax.dot_general(
            grad_tile[...], pads[s, :, r * LANES : r * LANES + CELLS], NT, preferred_element_type=F32
        )
        chans = term.shape[0]
        for part in range(2):
            rows = slice((2 * tap + part) * chans, (2 * tap + part + 1) * chans)
            piece = term[:, part * LANES : (part + 1) * LANES]
            out[rows] = piece
            out_low[rows] = piece.astype(BF16)


def grad_two_kernel(flips, act, cotangent, *refs):
    halo, pads, outs = (refs[:4], refs[4], refs[5:])
    pad_forward(pads, act[...], edge_flags(flips), halo)
    grad_kernel(cotangent, pads, *outs)


def result_kernel(flips, field, cotangent, back, one, two, pads, *refs):
    halo, (output, grad_fields, back_pads) = (refs[:4], refs[4:])
    flags = edge_flags(flips)
    total = (field[...].astype(F32) + conv(two, pads)).astype(BF16)
    pad_backward(back_pads, back[...], flags, halo)
    grads = (cotangent[...].astype(F32) + conv_adjoint(one, back_pads, flags, halo)).astype(BF16)
    for row in range(ROWS):
        span = slice(row * LANES, (row + 1) * LANES)
        output[:, row, :] = total[:, span]
        grad_fields[:, row, :] = grads[:, span]


def finish_kernel(mine, beside, paired, across, out_one, out_two):
    place = lax.axis_index("dp")
    core, side = (lax.rem(place, 2) == 1, place >= 2)
    chans = out_one.shape[1]
    for group in range(mine.shape[0] // chans):
        rows = slice(group * chans, (group + 1) * chans)
        a, b, c, d = (ref[rows].astype(F32) for ref in (mine, beside, paired, across))
        near, far = (jnp.where(core, c, a), jnp.where(core, d, b))
        low_one, high_one = (jnp.where(side, far, near), jnp.where(side, near, far))
        near, far = (jnp.where(core, a, c), jnp.where(core, b, d))
        low_two, high_two = (jnp.where(side, far, near), jnp.where(side, near, far))
        for out, pieces in ((out_one, (low_one, high_one)), (out_two, (low_two, high_two))):
            for half, piece in enumerate(pieces):
                tap, part = divmod(group + half * 9, 2)
                out[tap, :, part * LANES : (part + 1) * LANES] = piece


SMEM = pl.BlockSpec(memory_space=pltpu.SMEM)
VMEM = pl.BlockSpec(memory_space=pltpu.VMEM)


def call(kernel, name, out_shape, args, scratch=(), flags=True):
    return pl.pallas_call(
        kernel,
        name=name,
        out_shape=out_shape,
        in_specs=([SMEM] if flags else []) + [VMEM] * (len(args) - (1 if flags else 0)),
        out_specs=jax.tree.map(lambda _: VMEM, out_shape),
        scratch_shapes=list(scratch),
        compiler_params=pltpu.CompilerParams(vmem_limit_bytes=56 * 1024 * 1024),
    )(*args)


def struct(*shape, dtype=BF16):
    return jax.ShapeDtypeStruct(shape, dtype)


def rim_shapes(chans):
    side = struct(4 * ROWS, chans)
    line = struct(2 * chans, LANES)
    return (side, side, line, line)


def exchange(rim):
    east, west, south, north = rim
    lons, lats = (lax.axis_size("lon"), lax.axis_size("lat"))

    def along(value, step):
        return lax.ppermute(value, "lon", [(i, (i + step) % lons) for i in range(lons)])

    def across(value, step):
        return lax.ppermute(
            value, "lat", [(i, i + step) for i in range(lats) if 0 <= i + step < lats]
        )

    from_w, from_e = (along(east, 1), along(west, -1))
    line = struct(south.shape[0] + 32, LANES)
    south, north = call(join_kernel, "join", (line, line), (south, north, from_w, from_e), flags=False)
    return (from_w, from_e, across(south, 1), across(north, -1))


def beside(value):
    return lax.ppermute(value, "dp", [(i, (i + 2) % 4) for i in range(4)])


def paired(value):
    return lax.ppermute(value, "dp", [(0, 1), (1, 0), (2, 3), (3, 2)])


def reduce_grads(one, two):
    (one, one_low), (two, two_low) = (one, two)
    place = lax.axis_index("dp")
    core, side = (place % 2, place // 2)
    got_one = lax.ppermute(one_low, "dp", [(1, 0), (3, 2)])
    got_two = lax.ppermute(two_low, "dp", [(0, 1), (2, 3)])
    mine = jnp.where(core == 0, one + got_one.astype(F32), two + got_two.astype(F32))
    half = mine.shape[0] // 2
    away = lax.dynamic_slice_in_dim(mine, (1 - side) * half, half, 0).astype(BF16)
    kept = lax.dynamic_slice_in_dim(mine, side * half, half, 0)
    tiles = lax.axis_size("lon") * lax.axis_size("lat")
    part = (kept + beside(away).astype(F32)).astype(BF16).reshape(tiles, half // tiles, LANES)
    part = lax.all_to_all(part, ("lon", "lat"), 0, 0)
    total = jnp.sum(part.astype(F32), 0).astype(BF16)
    part = lax.all_to_all(jnp.broadcast_to(total[None], part.shape), ("lon", "lat"), 0, 0)
    part = part.reshape(half, LANES)
    other = beside(part)
    return (part, other, paired(part), paired(other))


def per_device(fields, weight_one, weight_two, edge_flips, cotangent):
    chans = fields.shape[1]
    tile = struct(chans, ROWS, LANES)
    flat = struct(chans, CELLS)
    pads = struct(3, chans, PADDED)
    scratch = [pltpu.VMEM((3, chans, PADDED), BF16)]
    field, cot, *rim = call(
        prepare_kernel,
        "prepare",
        (flat, flat) + rim_shapes(chans),
        (edge_flips, fields.reshape(tile.shape), cotangent.reshape(tile.shape)),
    )
    halo = exchange(rim)
    act, back, pads_in, *rim = call(
        hidden_kernel,
        "hidden",
        (flat, flat, pads) + rim_shapes(chans),
        (edge_flips, field, cot, weight_one, weight_two) + halo,
        scratch,
    )
    halo = exchange(rim)
    local = (struct(18 * chans, LANES, dtype=F32), struct(18 * chans, LANES))
    local_one = call(grad_kernel, "grad_one", local, (back, pads_in), flags=False)
    pads_act, *local_two = call(
        grad_two_kernel, "grad_two", (pads,) + local, (edge_flips, act, cot) + halo
    )
    quarters = reduce_grads(local_one, local_two)
    output, grad_fields = call(
        result_kernel,
        "result",
        (tile, tile),
        (edge_flips, field, cot, back, weight_one, weight_two, pads_act) + halo,
        scratch,
    )
    grad = struct(9, chans, chans, dtype=F32)
    grad_one, grad_two = call(finish_kernel, "finish", (grad, grad), quarters, flags=False)
    return (output.reshape(fields.shape), grad_fields.reshape(fields.shape), grad_one, grad_two)


def solution(mesh):
    in_specs = (P("dp", None, "lat", "lon"), P(), P(), P(), P("dp", None, "lat", "lon"))
    out_specs = (P("dp", None, "lat", "lon"), P("dp", None, "lat", "lon"), P(), P())
    return jax.shard_map(
        per_device, mesh=mesh, in_specs=in_specs, out_specs=out_specs, check_vma=False
    )
```

```python
import jax
import jax.numpy as jnp
from jax import lax
from jax.experimental import pallas as pl
from jax.experimental.pallas import tpu as pltpu
from jax.sharding import PartitionSpec as P


F32 = jnp.float32
BF16 = jnp.bfloat16
LANES = 128
ROWS = 8
CELLS = ROWS * LANES
PADDED = CELLS + 2 * LANES
NT = (((1,), (1,)), ((), ()))
TN = (((0,), (0,)), ((), ()))


def iota(shape, dim):
    return lax.broadcasted_iota(jnp.int32, shape, dim)


def one_hot(cond):
    return jnp.where(cond, 1.0, 0.0).astype(BF16)


def dot(a, b):
    return jnp.dot(a, b, preferred_element_type=F32)


def edge_flags(flips):
    a, o = (lax.axis_index("lat"), lax.axis_index("lon"))
    edges, lons = flips.shape

    def upper(col):
        return jnp.where(a > 0, flips[jnp.maximum(a - 1, 0), col], 0)

    def lower(col):
        return jnp.where(a < edges, flips[jnp.minimum(a, edges - 1), col], 0)

    west, east = (lax.rem(o + lons - 1, lons), lax.rem(o + 1, lons))
    return (upper(o), lower(o), upper(west), upper(east), lower(west), lower(east))


def rims(first, second, flags, outs):
    east, west, south, north = outs
    shape = (2 * ROWS, CELLS)
    row, cell = (iota(shape, 0), iota(shape, 1))
    pick = one_hot(cell == jnp.where(row < ROWS, row * LANES + LANES - 1, (row - ROWS) * LANES))
    one = lax.dot_general(pick, first, NT, preferred_element_type=F32)
    two = lax.dot_general(pick, second, NT, preferred_element_type=F32)
    chans = first.shape[0]
    upper, lower = (flags[0] == 1, flags[1] == 1)
    end = ROWS - 1

    def side(out, base, far):
        top = jnp.where(upper, two[far : far + 1], two[base : base + 1])
        low = jnp.where(lower, two[far + end : far + ROWS], two[base + end : base + ROWS])
        at = iota((ROWS, chans), 0)
        corners = jnp.where(at == 0, jnp.broadcast_to(top, at.shape), jnp.broadcast_to(low, at.shape))
        out[...] = jnp.concatenate(
            [one[base : base + ROWS], two[base : base + ROWS], corners, corners], 0
        ).astype(BF16)

    side(east, 0, ROWS)
    side(west, ROWS, 0)
    south[:chans] = first[:, CELLS - LANES :]
    south[chans:] = second[:, CELLS - LANES :]
    north[:chans] = first[:, :LANES]
    north[chans:] = second[:, :LANES]


def join_kernel(south, north, from_w, from_e, south_out, north_out):
    rows = south.shape[0]
    west, east = (from_w[...].astype(F32), from_e[...].astype(F32))
    at = iota((16, west.shape[1]), 0)
    for rim, out, near, corner in ((south, south_out, 7, 17), (north, north_out, 0, 16)):
        out[:rows] = rim[...]
        spread = [
            jnp.broadcast_to(side[k : k + 1], at.shape)
            for side in (west, east)
            for k in (near, corner)
        ]
        block = jnp.where(
            at == 0, spread[0], jnp.where(at == 1, spread[1], jnp.where(at == 2, spread[2], spread[3]))
        ).astype(BF16)
        out[rows : rows + 16] = block[:, :LANES]
        out[rows + 16 :] = block[:, LANES:]


def corners_of(line, chans):
    rows = 2 * chans
    return jnp.concatenate([line[rows : rows + 16], line[rows + 16 : rows + 32]], 1)


def turned(line, flip):
    shape = (LANES, LANES)
    a, b = (iota(shape, 0), iota(shape, 1))
    turn = one_hot(b == a + flip * (LANES - 1 - 2 * a))
    return dot(line, turn)


def shifted(out, centre, top, bottom, west, east, swap_top=None, swap_bottom=None):
    chans = centre.shape[0]
    k, lane = (iota((16, PADDED), 0), iota((16, PADDED), 1))
    placed_west = lax.dot_general(
        west, one_hot(lane == k * LANES), TN, preferred_element_type=F32
    )
    placed_east = lax.dot_general(
        east, one_hot(lane == k * LANES + LANES - 1), TN, preferred_element_type=F32
    )
    lane_in = iota((chans, LANES), 1)
    for block in range(ROWS + 2):
        span = slice(block * LANES, (block + 1) * LANES)
        if block == 0:
            line = top
        elif block == ROWS + 1:
            line = bottom
        else:
            line = centre[:, (block - 1) * LANES : block * LANES].astype(F32)
        left = jnp.where(lane_in == 0, placed_west[:, span], pltpu.roll(line, 1, 1))
        right = jnp.where(lane_in == LANES - 1, placed_east[:, span], pltpu.roll(line, LANES - 1, 1))
        swap = swap_top if block == 0 else swap_bottom if block == ROWS + 1 else None
        if swap is not None:
            left, right = (jnp.where(swap, right, left), jnp.where(swap, left, right))
        out[0, :, span] = left.astype(BF16)
        out[1, :, span] = line.astype(BF16)
        out[2, :, span] = right.astype(BF16)


def lines(top, mid, bottom):
    return jnp.concatenate([top, mid, bottom, jnp.zeros((6, mid.shape[1]), F32)], 0).astype(BF16)


def pad_forward(out, centre, flags, halo):
    from_w, from_e, from_n, from_s = halo
    chans = centre.shape[0]
    upper, lower = (flags[0] == 1, flags[1] == 1)
    above, below = (corners_of(ref, chans).astype(F32) for ref in (from_n, from_s))
    nw, ne, sw, se = (above[:1], above[2:3], below[:1], below[2:3])
    west = lines(jnp.where(upper, ne, nw), from_w[...].astype(F32)[:ROWS], jnp.where(lower, se, sw))
    east = lines(jnp.where(upper, nw, ne), from_e[...].astype(F32)[:ROWS], jnp.where(lower, sw, se))
    top = turned(from_n[:chans], flags[0])
    bottom = turned(from_s[:chans], flags[1])
    shifted(out, centre, top, bottom, west, east)


def pad_backward(out, centre, flags, halo):
    from_w, from_e, from_n, from_s = halo
    chans = centre.shape[0]
    upper, lower = (flags[0] == 1, flags[1] == 1)
    none = jnp.zeros((1, chans), F32)
    west = lines(none, from_w[...].astype(F32)[ROWS : 2 * ROWS], none)
    east = lines(none, from_e[...].astype(F32)[ROWS : 2 * ROWS], none)
    top = turned(from_n[chans : 2 * chans], flags[0])
    bottom = turned(from_s[chans : 2 * chans], flags[1])
    shifted(out, centre, top, bottom, west, east, upper, lower)


def conv(weight, pads):
    total = None
    for tap in range(9):
        r, s = divmod(tap, 3)
        term = dot(weight[tap], pads[s, :, r * LANES : r * LANES + CELLS])
        total = term if total is None else total + term
    return total


def conv_adjoint(weight, pads, flags, halo):
    total = None
    for tap in range(9):
        r, s = divmod(tap, 3)
        start = (2 - r) * LANES
        term = lax.dot_general(
            weight[tap], pads[2 - s, :, start : start + CELLS], TN, preferred_element_type=F32
        )
        total = term if total is None else total + term
    chans = total.shape[0]
    above, below = (corners_of(ref, chans) for ref in halo[2:])
    k, lane = (iota((16, LANES), 0), iota((16, LANES), 1))

    def corner(block, which, at, tap):
        spread = lax.dot_general(
            block, one_hot((k == which) & (lane == at)), TN, preferred_element_type=F32
        ).astype(BF16)
        return lax.dot_general(weight[tap], spread, TN, preferred_element_type=F32)

    east = LANES - 1
    top = corner(above, 1, 0, 8 - 2 * flags[2]) + corner(above, 3, east, 6 + 2 * flags[3])
    bottom = corner(below, 1, 0, 2 - 2 * flags[4]) + corner(below, 3, east, 2 * flags[5])
    return jnp.concatenate(
        [total[:, :LANES] + top, total[:, LANES : CELLS - LANES], total[:, CELLS - LANES :] + bottom],
        1,
    )


def prepare_kernel(flips, field, cotangent, *outs):
    flat_field, flat_cot = outs[:2]
    for row in range(ROWS):
        span = slice(row * LANES, (row + 1) * LANES)
        flat_field[:, span] = field[:, row, :]
        flat_cot[:, span] = cotangent[:, row, :]
    rims(flat_field[...], flat_cot[...], edge_flags(flips), outs[2:])


def hidden_kernel(flips, field, cotangent, one, two, *refs):
    halo, outs, back_pads = (refs[:4], refs[4:-1], refs[-1])
    act_out, back_out, pads = outs[:3]
    flags = edge_flags(flips)
    pad_forward(pads, field[...], flags, halo)
    pad_backward(back_pads, cotangent[...], flags, halo)
    hidden = conv(one, pads)
    back_act = conv_adjoint(two, back_pads, flags, halo)
    sigma = 1.0 / (1.0 + jnp.exp(-hidden))
    act_out[...] = (hidden * sigma).astype(BF16)
    back_out[...] = (back_act * sigma * (1.0 + hidden * (1.0 - sigma))).astype(BF16)
    rims(act_out[...], back_out[...], flags, outs[3:])


def grad_kernel(grad_tile, pads, keep, away):
    core = lax.rem(lax.axis_index("dp"), 2)
    for tap in range(9):
        r, s = divmod(tap, 3)
        term = lax.dot_general(
            grad_tile[...], pads[s, :, r * LANES : r * LANES + CELLS], NT, preferred_element_type=F32
        )
        for part in range(2):
            half, group = divmod(2 * tap + part, 9)
            sides, tiles, rows, lanes = keep.shape
            shape = (sides, tiles, rows // 9, lanes)
            piece = term[:, part * LANES : (part + 1) * LANES].reshape(shape)
            span = slice(group * shape[2], (group + 1) * shape[2])

            @pl.when(core == half)
            def _():
                keep[:, :, span, :] = piece

            @pl.when(core != half)
            def _():
                away[:, :, span, :] = piece.astype(BF16)


def fold_kernel(keep, got, kept, away):
    side = lax.div(lax.axis_index("dp"), 2)
    kept[...] = keep[side] + got[side].astype(F32)
    away[...] = (keep[1 - side] + got[1 - side].astype(F32)).astype(BF16)


def grad_two_kernel(flips, act, cotangent, *refs):
    halo, pads, outs = (refs[:4], refs[4], refs[5:])
    pad_forward(pads, act[...], edge_flags(flips), halo)
    grad_kernel(cotangent, pads, *outs)


def result_kernel(flips, field, cotangent, back, one, two, pads, *refs):
    halo, (output, grad_fields, back_pads) = (refs[:4], refs[4:])
    flags = edge_flags(flips)
    total = (field[...].astype(F32) + conv(two, pads)).astype(BF16)
    pad_backward(back_pads, back[...], flags, halo)
    grads = (cotangent[...].astype(F32) + conv_adjoint(one, back_pads, flags, halo)).astype(BF16)
    for row in range(ROWS):
        span = slice(row * LANES, (row + 1) * LANES)
        output[:, row, :] = total[:, span]
        grad_fields[:, row, :] = grads[:, span]


def finish_kernel(mine, beside, paired, across, out_one, out_two):
    place = lax.axis_index("dp")
    core, side = (lax.rem(place, 2) == 1, place >= 2)
    rows = out_one.shape[1] // 2
    _, depth = mine.shape[:2]
    thick = depth // 18
    for which, out in enumerate((out_one, out_two)):
        for group in range(9):
            start = (which * 9 + group) * thick
            a, b, c, d = (
                ref[:, start : start + thick, :].astype(F32).reshape(rows, LANES)
                for ref in (mine, beside, paired, across)
            )
            for half in range(2):
                tap, part = divmod(group + half * 9, 2)
                other = core if half == 0 else jnp.logical_not(core)
                near, far = (jnp.where(other, c, a), jnp.where(other, d, b))
                lanes = slice(part * LANES, (part + 1) * LANES)
                out[tap, :rows, lanes] = jnp.where(side, far, near)
                out[tap, rows:, lanes] = jnp.where(side, near, far)


SMEM = pl.BlockSpec(memory_space=pltpu.SMEM)
VMEM = pl.BlockSpec(memory_space=pltpu.VMEM)


def call(kernel, out_shape, args, scratch=(), flags=True):
    return pl.pallas_call(
        kernel,
        out_shape=out_shape,
        in_specs=([SMEM] if flags else []) + [VMEM] * (len(args) - (1 if flags else 0)),
        out_specs=jax.tree.map(lambda _: VMEM, out_shape),
        scratch_shapes=list(scratch),
        compiler_params=pltpu.CompilerParams(vmem_limit_bytes=56 * 1024 * 1024),
    )(*args)


def struct(*shape, dtype=BF16):
    return jax.ShapeDtypeStruct(shape, dtype)


def rim_shapes(chans):
    side = struct(4 * ROWS, chans)
    line = struct(2 * chans, LANES)
    return (side, side, line, line)


def exchange(rim):
    east, west, south, north = rim
    lons, lats = (lax.axis_size("lon"), lax.axis_size("lat"))

    def along(value, step):
        return lax.ppermute(value, "lon", [(i, (i + step) % lons) for i in range(lons)])

    def across(value, step):
        return lax.ppermute(
            value, "lat", [(i, i + step) for i in range(lats) if 0 <= i + step < lats]
        )

    from_w, from_e = (along(east, 1), along(west, -1))
    line = struct(south.shape[0] + 32, LANES)
    south, north = call(join_kernel, (line, line), (south, north, from_w, from_e), flags=False)
    from_n = across(south, 1)
    from_s = across(north, -1)
    return (from_w, from_e, from_n, from_s)


def beside(value):
    return lax.ppermute(value, "dp", [(i, (i + 2) % 4) for i in range(4)])


def paired(value):
    return lax.ppermute(value, "dp", [(0, 1), (1, 0), (2, 3), (3, 2)])


def over(value, axis):
    return lax.all_to_all(value, axis, 0, 0)


def total(parts):
    return jnp.sum(parts.astype(F32), 0)


def fold(grad):
    keep, away = grad
    shape = keep.shape[1:]
    return call(fold_kernel, (struct(*shape, dtype=F32), struct(*shape)), (keep, paired(away)), flags=False)


def lat_sum(kept, away):
    got = beside(away)
    return total(over((kept + got.astype(F32)).astype(BF16), "lat"))


def gathered(value, axis):
    return over(jnp.broadcast_to(value[None], (lax.axis_size(axis),) + value.shape), axis)


def reduce_grads(one, two):
    share = jnp.concatenate([lat_sum(*one), lat_sum(*two)], 0)
    lons = lax.axis_size("lon")
    share = total(over(share.reshape(lons, share.shape[0] // lons, LANES), "lon")).astype(BF16)
    share = gathered(share, "lon")
    return gathered(share.reshape(-1, LANES), "lat")


def per_device(fields, weight_one, weight_two, edge_flips, cotangent):
    chans = fields.shape[1]
    tile = struct(chans, ROWS, LANES)
    flat = struct(chans, CELLS)
    pads = struct(3, chans, PADDED)
    scratch = [pltpu.VMEM((3, chans, PADDED), BF16)]
    field, cot, *rim = call(
        prepare_kernel,
        (flat, flat) + rim_shapes(chans),
        (edge_flips, fields.reshape(tile.shape), cotangent.reshape(tile.shape)),
    )
    halo = exchange(rim)
    act, back, pads_in, *rim = call(
        hidden_kernel,
        (flat, flat, pads) + rim_shapes(chans),
        (edge_flips, field, cot, weight_one, weight_two) + halo,
        scratch,
    )
    halo = exchange(rim)
    local = (2, lax.axis_size("lat"), 9 * chans // (2 * lax.axis_size("lat")), LANES)
    local = (struct(*local, dtype=F32), struct(*local))
    one = call(grad_kernel, local, (back, pads_in), flags=False)
    one = fold(one)
    act, _ = lax.optimization_barrier((act, one[0]))
    pads_act, *two = call(grad_two_kernel, (pads,) + local, (edge_flips, act, cot) + halo)
    quarter = reduce_grads(one, fold(two))
    quarter, back = lax.optimization_barrier((quarter, back))
    other = beside(quarter)
    output, grad_fields = call(
        result_kernel, (tile, tile), (edge_flips, field, cot, back, weight_one, weight_two, pads_act) + halo, scratch
    )
    grad = struct(9, chans, chans, dtype=F32)
    grad_one, grad_two = call(
        finish_kernel, (grad, grad), (quarter, other, paired(quarter), paired(other)), flags=False
    )
    return (output.reshape(fields.shape), grad_fields.reshape(fields.shape), grad_one, grad_two)


def solution(mesh):
    in_specs = (P("dp", None, "lat", "lon"), P(), P(), P(), P("dp", None, "lat", "lon"))
    out_specs = (P("dp", None, "lat", "lon"), P("dp", None, "lat", "lon"), P(), P())


    return jax.shard_map(per_device, mesh=mesh, in_specs=in_specs, out_specs=out_specs, check_vma=False)
```

```python
import jax
import jax.numpy as jnp
from jax import lax
from jax.experimental import pallas as pl
from jax.experimental.pallas import tpu as pltpu
from jax.sharding import PartitionSpec as P


F32 = jnp.float32
BF16 = jnp.bfloat16
LANES = 128
ROWS = 8
CELLS = ROWS * LANES
PADDED = CELLS + 2 * LANES
NT = (((1,), (1,)), ((), ()))
TN = (((0,), (0,)), ((), ()))


def iota(shape, dim):
    return lax.broadcasted_iota(jnp.int32, shape, dim)


def one_hot(cond):
    return jnp.where(cond, 1.0, 0.0).astype(BF16)


def dot(a, b):
    return jnp.dot(a, b, preferred_element_type=F32)


def edge_flags(flips):
    a, o = (lax.axis_index("lat"), lax.axis_index("lon"))
    edges, lons = flips.shape

    def upper(col):
        return jnp.where(a > 0, flips[jnp.maximum(a - 1, 0), col], 0)

    def lower(col):
        return jnp.where(a < edges, flips[jnp.minimum(a, edges - 1), col], 0)

    west, east = (lax.rem(o + lons - 1, lons), lax.rem(o + 1, lons))
    return (upper(o), lower(o), upper(west), upper(east), lower(west), lower(east))


def rims(first, second, flags, outs):
    east, west, south, north = outs
    shape = (2 * ROWS, CELLS)
    row, cell = (iota(shape, 0), iota(shape, 1))
    pick = one_hot(cell == jnp.where(row < ROWS, row * LANES + LANES - 1, (row - ROWS) * LANES))
    one = lax.dot_general(pick, first, NT, preferred_element_type=F32)
    two = lax.dot_general(pick, second, NT, preferred_element_type=F32)
    chans = first.shape[0]
    upper, lower = (flags[0] == 1, flags[1] == 1)
    end = ROWS - 1

    def side(out, base, far):
        top = jnp.where(upper, two[far : far + 1], two[base : base + 1])
        low = jnp.where(lower, two[far + end : far + ROWS], two[base + end : base + ROWS])
        at = iota((ROWS, chans), 0)
        corners = jnp.where(at == 0, jnp.broadcast_to(top, at.shape), jnp.broadcast_to(low, at.shape))
        out[...] = jnp.concatenate(
            [one[base : base + ROWS], two[base : base + ROWS], corners, corners], 0
        ).astype(BF16)

    side(east, 0, ROWS)
    side(west, ROWS, 0)
    south[:chans] = first[:, CELLS - LANES :]
    south[chans:] = second[:, CELLS - LANES :]
    north[:chans] = first[:, :LANES]
    north[chans:] = second[:, :LANES]


def join_kernel(south, north, from_w, from_e, south_out, north_out):
    rows = south.shape[0]
    west, east = (from_w[...].astype(F32), from_e[...].astype(F32))
    at = iota((16, west.shape[1]), 0)
    for rim, out, near, corner in ((south, south_out, 7, 17), (north, north_out, 0, 16)):
        out[:rows] = rim[...]
        spread = [
            jnp.broadcast_to(side[k : k + 1], at.shape)
            for side in (west, east)
            for k in (near, corner)
        ]
        block = jnp.where(
            at == 0, spread[0], jnp.where(at == 1, spread[1], jnp.where(at == 2, spread[2], spread[3]))
        ).astype(BF16)
        out[rows : rows + 16] = block[:, :LANES]
        out[rows + 16 :] = block[:, LANES:]


def corners_of(line, chans):
    rows = 2 * chans
    return jnp.concatenate([line[rows : rows + 16], line[rows + 16 : rows + 32]], 1)


def turned(line, flip):
    shape = (LANES, LANES)
    a, b = (iota(shape, 0), iota(shape, 1))
    turn = one_hot(b == a + flip * (LANES - 1 - 2 * a))
    return dot(line, turn)


def shifted(out, centre, top, bottom, west, east, swap_top=None, swap_bottom=None):
    chans = centre.shape[0]
    k, lane = (iota((16, PADDED), 0), iota((16, PADDED), 1))
    placed_west = lax.dot_general(
        west, one_hot(lane == k * LANES), TN, preferred_element_type=F32
    )
    placed_east = lax.dot_general(
        east, one_hot(lane == k * LANES + LANES - 1), TN, preferred_element_type=F32
    )
    lane_in = iota((chans, LANES), 1)
    for block in range(ROWS + 2):
        span = slice(block * LANES, (block + 1) * LANES)
        if block == 0:
            line = top
        elif block == ROWS + 1:
            line = bottom
        else:
            line = centre[:, (block - 1) * LANES : block * LANES].astype(F32)
        left = jnp.where(lane_in == 0, placed_west[:, span], pltpu.roll(line, 1, 1))
        right = jnp.where(lane_in == LANES - 1, placed_east[:, span], pltpu.roll(line, LANES - 1, 1))
        swap = swap_top if block == 0 else swap_bottom if block == ROWS + 1 else None
        if swap is not None:
            left, right = (jnp.where(swap, right, left), jnp.where(swap, left, right))
        out[0, :, span] = left.astype(BF16)
        out[1, :, span] = line.astype(BF16)
        out[2, :, span] = right.astype(BF16)


def lines(top, mid, bottom):
    return jnp.concatenate([top, mid, bottom, jnp.zeros((6, mid.shape[1]), F32)], 0).astype(BF16)


def pad_forward(out, centre, flags, halo):
    from_w, from_e, from_n, from_s = halo
    chans = centre.shape[0]
    upper, lower = (flags[0] == 1, flags[1] == 1)
    above, below = (corners_of(ref, chans).astype(F32) for ref in (from_n, from_s))
    nw, ne, sw, se = (above[:1], above[2:3], below[:1], below[2:3])
    west = lines(jnp.where(upper, ne, nw), from_w[...].astype(F32)[:ROWS], jnp.where(lower, se, sw))
    east = lines(jnp.where(upper, nw, ne), from_e[...].astype(F32)[:ROWS], jnp.where(lower, sw, se))
    top = turned(from_n[:chans], flags[0])
    bottom = turned(from_s[:chans], flags[1])
    shifted(out, centre, top, bottom, west, east)


def pad_backward(out, centre, flags, halo):
    from_w, from_e, from_n, from_s = halo
    chans = centre.shape[0]
    upper, lower = (flags[0] == 1, flags[1] == 1)
    none = jnp.zeros((1, chans), F32)
    west = lines(none, from_w[...].astype(F32)[ROWS : 2 * ROWS], none)
    east = lines(none, from_e[...].astype(F32)[ROWS : 2 * ROWS], none)
    top = turned(from_n[chans : 2 * chans], flags[0])
    bottom = turned(from_s[chans : 2 * chans], flags[1])
    shifted(out, centre, top, bottom, west, east, upper, lower)


def conv(weight, pads):
    total = None
    for tap in range(9):
        r, s = divmod(tap, 3)
        term = dot(weight[tap], pads[s, :, r * LANES : r * LANES + CELLS])
        total = term if total is None else total + term
    return total


def conv_adjoint(weight, pads, flags, halo):
    total = None
    for tap in range(9):
        r, s = divmod(tap, 3)
        start = (2 - r) * LANES
        term = lax.dot_general(
            weight[tap], pads[2 - s, :, start : start + CELLS], TN, preferred_element_type=F32
        )
        total = term if total is None else total + term
    chans = total.shape[0]
    above, below = (corners_of(ref, chans) for ref in halo[2:])
    k, lane = (iota((16, LANES), 0), iota((16, LANES), 1))

    def corner(block, which, at, tap):
        spread = lax.dot_general(
            block, one_hot((k == which) & (lane == at)), TN, preferred_element_type=F32
        ).astype(BF16)
        return lax.dot_general(weight[tap], spread, TN, preferred_element_type=F32)

    east = LANES - 1
    top = corner(above, 1, 0, 8 - 2 * flags[2]) + corner(above, 3, east, 6 + 2 * flags[3])
    bottom = corner(below, 1, 0, 2 - 2 * flags[4]) + corner(below, 3, east, 2 * flags[5])
    return jnp.concatenate(
        [total[:, :LANES] + top, total[:, LANES : CELLS - LANES], total[:, CELLS - LANES :] + bottom],
        1,
    )


def prepare_kernel(flips, field, cotangent, *outs):
    flat_field, flat_cot = outs[:2]
    for row in range(ROWS):
        span = slice(row * LANES, (row + 1) * LANES)
        flat_field[:, span] = field[:, row, :]
        flat_cot[:, span] = cotangent[:, row, :]
    rims(flat_field[...], flat_cot[...], edge_flags(flips), outs[2:])


def hidden_kernel(flips, field, cotangent, one, two, *refs):
    halo, outs, back_pads = (refs[:4], refs[4:-1], refs[-1])
    act_out, back_out, pads = outs[:3]
    flags = edge_flags(flips)
    pad_forward(pads, field[...], flags, halo)
    pad_backward(back_pads, cotangent[...], flags, halo)
    hidden = conv(one, pads)
    back_act = conv_adjoint(two, back_pads, flags, halo)
    sigma = 1.0 / (1.0 + jnp.exp(-hidden))
    act_out[...] = (hidden * sigma).astype(BF16)
    back_out[...] = (back_act * sigma * (1.0 + hidden * (1.0 - sigma))).astype(BF16)
    rims(act_out[...], back_out[...], flags, outs[3:])


def grad_kernel(grad_tile, pads, keep, away):
    core = lax.rem(lax.axis_index("dp"), 2)
    for tap in range(9):
        r, s = divmod(tap, 3)
        term = lax.dot_general(
            grad_tile[...], pads[s, :, r * LANES : r * LANES + CELLS], NT, preferred_element_type=F32
        )
        chans = term.shape[0]
        for part in range(2):
            half, group = divmod(2 * tap + part, 9)
            piece = term[:, part * LANES : (part + 1) * LANES]
            rows = slice(group * chans, (group + 1) * chans)

            @pl.when(core == half)
            def _():
                keep[rows] = piece

            @pl.when(core != half)
            def _():
                away[rows] = piece.astype(BF16)


def grad_two_kernel(flips, act, cotangent, *refs):
    halo, pads, outs = (refs[:4], refs[4], refs[5:])
    pad_forward(pads, act[...], edge_flags(flips), halo)
    grad_kernel(cotangent, pads, *outs)


def output_kernel(field, weight, pads, output):
    total = (field[...].astype(F32) + conv(weight, pads)).astype(BF16)
    for row in range(ROWS):
        output[:, row, :] = total[:, row * LANES : (row + 1) * LANES]


def grad_fields_kernel(flips, cotangent, back, weight, *refs):
    halo, (grad_fields, back_pads) = (refs[:4], refs[4:])
    flags = edge_flags(flips)
    pad_backward(back_pads, back[...], flags, halo)
    total = (cotangent[...].astype(F32) + conv_adjoint(weight, back_pads, flags, halo)).astype(BF16)
    for row in range(ROWS):
        grad_fields[:, row, :] = total[:, row * LANES : (row + 1) * LANES]


def finish_kernel(mine, beside, paired, across, out_one, out_two, flat):
    place = lax.axis_index("dp")
    core, side = (lax.rem(place, 2) == 1, place >= 2)
    chans = out_one.shape[1]
    tiles, depth = mine.shape[:2]
    depth = depth // 2
    for which, out in enumerate((out_one, out_two)):
        for tile in range(tiles):
            a, b, c, d = (
                ref[tile, which * depth : (which + 1) * depth, :]
                for ref in (mine, beside, paired, across)
            )
            low, high = (tile * depth, (tiles + tile) * depth)
            for half, (near, far) in enumerate(((a, b), (c, d))):
                flat[half, low : low + depth] = jnp.where(side, far, near)
                flat[half, high : high + depth] = jnp.where(side, near, far)
        for group in range(9):
            rows = slice(group * chans, (group + 1) * chans)
            own, other = (flat[0, rows].astype(F32), flat[1, rows].astype(F32))
            for half in range(2):
                tap, part = divmod(group + half * 9, 2)
                piece = jnp.where(core, other, own) if half == 0 else jnp.where(core, own, other)
                out[tap, :, part * LANES : (part + 1) * LANES] = piece


SMEM = pl.BlockSpec(memory_space=pltpu.SMEM)
VMEM = pl.BlockSpec(memory_space=pltpu.VMEM)


def call(kernel, out_shape, args, scratch=(), flags=True):
    return pl.pallas_call(
        kernel,
        out_shape=out_shape,
        in_specs=([SMEM] if flags else []) + [VMEM] * (len(args) - (1 if flags else 0)),
        out_specs=jax.tree.map(lambda _: VMEM, out_shape),
        scratch_shapes=list(scratch),
        compiler_params=pltpu.CompilerParams(vmem_limit_bytes=56 * 1024 * 1024),
    )(*args)


def struct(*shape, dtype=BF16):
    return jax.ShapeDtypeStruct(shape, dtype)


def rim_shapes(chans):
    side = struct(4 * ROWS, chans)
    line = struct(2 * chans, LANES)
    return (side, side, line, line)


def exchange(rim):
    east, west, south, north = rim
    lons, lats = (lax.axis_size("lon"), lax.axis_size("lat"))

    def along(value, step):
        return lax.ppermute(value, "lon", [(i, (i + step) % lons) for i in range(lons)])

    def across(value, step):
        return lax.ppermute(
            value, "lat", [(i, i + step) for i in range(lats) if 0 <= i + step < lats]
        )

    from_w, from_e = (along(east, 1), along(west, -1))
    line = struct(south.shape[0] + 32, LANES)
    south, north = call(join_kernel, (line, line), (south, north, from_w, from_e), flags=False)
    from_n = across(south, 1)
    from_s = across(north, -1)
    return (from_w, from_e, from_n, from_s)


def beside(value):
    return lax.ppermute(value, "dp", [(i, (i + 2) % 4) for i in range(4)])


def paired(value):
    return lax.ppermute(value, "dp", [(0, 1), (1, 0), (2, 3), (3, 2)])


def over(value, axis):
    return lax.all_to_all(value, axis, 0, 0)


def total(parts):
    return jnp.sum(parts.astype(F32), 0)


def fold(grad):
    keep, away = grad
    got = paired(away)
    side = lax.shift_right_logical(lax.axis_index("dp"), 1)
    half = keep.shape[0] // 2

    def rows(which):
        pick = lambda value: lax.dynamic_slice_in_dim(value, which * half, half, 0).astype(F32)
        return pick(keep) + pick(got)

    return (rows(side), beside(rows(1 - side).astype(BF16)))


def gathered(value, axis):
    return over(jnp.broadcast_to(value[None], (lax.axis_size(axis),) + value.shape), axis)


def reduce_grads(one, two):
    lats, lons = (lax.axis_size("lat"), lax.axis_size("lon"))
    parts = [
        (kept + got.astype(F32)).astype(BF16).reshape(lats, -1, LANES) for kept, got in (one, two)
    ]
    share = total(over(jnp.concatenate(parts, 1), "lat"))
    share = total(over(share.reshape(lons, share.shape[0] // lons, LANES), "lon")).astype(BF16)
    share = gathered(share, "lon")
    return gathered(share.reshape(-1, LANES), "lat")


def per_device(fields, weight_one, weight_two, edge_flips, cotangent):
    chans = fields.shape[1]
    tile = struct(chans, ROWS, LANES)
    flat = struct(chans, CELLS)
    pads = struct(3, chans, PADDED)
    scratch = [pltpu.VMEM((3, chans, PADDED), BF16)]
    field, cot, *rim = call(
        prepare_kernel,
        (flat, flat) + rim_shapes(chans),
        (edge_flips, fields.reshape(tile.shape), cotangent.reshape(tile.shape)),
    )
    halo = exchange(rim)
    act, back, pads_in, *rim = call(
        hidden_kernel,
        (flat, flat, pads) + rim_shapes(chans),
        (edge_flips, field, cot, weight_one, weight_two) + halo,
        scratch,
    )
    halo = exchange(rim)
    local = (struct(9 * chans, LANES, dtype=F32), struct(9 * chans, LANES))
    one = call(grad_kernel, local, (back, pads_in), flags=False)
    one = fold(one)
    pads_act, *two = call(grad_two_kernel, (pads,) + local, (edge_flips, act, cot) + halo)
    two = fold(two)
    output = call(output_kernel, tile, (field, weight_two, pads_act), flags=False)
    quarter = reduce_grads(one, two)
    other = beside(quarter)
    grad_fields = call(
        grad_fields_kernel, tile, (edge_flips, cot, back, weight_one) + halo, scratch
    )
    grad = struct(9, chans, chans, dtype=F32)
    grad_one, grad_two = call(
        finish_kernel,
        (grad, grad),
        (quarter, other, paired(quarter), paired(other)),
        [pltpu.VMEM((2, 9 * chans, LANES), BF16)],
        flags=False,
    )
    return (output.reshape(fields.shape), grad_fields.reshape(fields.shape), grad_one, grad_two)


def solution(mesh):
    in_specs = (P("dp", None, "lat", "lon"), P(), P(), P(), P("dp", None, "lat", "lon"))
    out_specs = (P("dp", None, "lat", "lon"), P("dp", None, "lat", "lon"), P(), P())


    return jax.shard_map(
        per_device, mesh=mesh, in_specs=in_specs, out_specs=out_specs, check_vma=False
    )
```

```python
import functools

import jax
import jax.numpy as jnp
from jax import lax
from jax.experimental import pallas as pl
from jax.experimental.pallas import tpu as pltpu
from jax.sharding import PartitionSpec as P


F32 = jnp.float32
BF16 = jnp.bfloat16
LANES = 128
ROWS = 8
CELLS = ROWS * LANES
PADDED = CELLS + 2 * LANES
NT = (((1,), (1,)), ((), ()))
TN = (((0,), (0,)), ((), ()))


def iota(shape, dim):
    return lax.broadcasted_iota(jnp.int32, shape, dim)


def one_hot(cond):
    return jnp.where(cond, 1.0, 0.0).astype(BF16)


def dot(a, b):
    return jnp.dot(a, b, preferred_element_type=F32)


def edge_flags(flips):
    a, o = (lax.axis_index("lat"), lax.axis_index("lon"))
    edges, lons = flips.shape

    def upper(col):
        return jnp.where(a > 0, flips[jnp.maximum(a - 1, 0), col], 0)

    def lower(col):
        return jnp.where(a < edges, flips[jnp.minimum(a, edges - 1), col], 0)

    west, east = (lax.rem(o + lons - 1, lons), lax.rem(o + 1, lons))
    return (upper(o), lower(o), upper(west), upper(east), lower(west), lower(east))


def rims(first, second, flags, outs):
    east, west, south, north = outs
    shape = (2 * ROWS, CELLS)
    row, cell = (iota(shape, 0), iota(shape, 1))
    pick = one_hot(cell == jnp.where(row < ROWS, row * LANES + LANES - 1, (row - ROWS) * LANES))
    one = lax.dot_general(pick, first, NT, preferred_element_type=F32)
    two = lax.dot_general(pick, second, NT, preferred_element_type=F32)
    chans = first.shape[0]
    upper, lower = (flags[0] == 1, flags[1] == 1)
    end = ROWS - 1

    def side(out, base, far):
        top = jnp.where(upper, two[far : far + 1], two[base : base + 1])
        low = jnp.where(lower, two[far + end : far + ROWS], two[base + end : base + ROWS])
        at = iota((ROWS, chans), 0)
        corners = jnp.where(at == 0, jnp.broadcast_to(top, at.shape), jnp.broadcast_to(low, at.shape))
        out[...] = jnp.concatenate(
            [one[base : base + ROWS], two[base : base + ROWS], corners, corners], 0
        ).astype(BF16)

    side(east, 0, ROWS)
    side(west, ROWS, 0)
    south[:chans] = first[:, CELLS - LANES :]
    south[chans : 2 * chans] = second[:, CELLS - LANES :]
    north[:chans] = first[:, :LANES]
    north[chans : 2 * chans] = second[:, :LANES]


def join_kernel(south, north, from_w, from_e, south_out, north_out, block, sems):
    rows = south_out.shape[0] - 32
    west, east = (from_w[...].astype(F32), from_e[...].astype(F32))
    at = iota((16, west.shape[1]), 0)
    copies = []
    for index, (out, near, corner) in enumerate(((south_out, 7, 17), (north_out, 0, 16))):
        spread = [
            jnp.broadcast_to(side[k : k + 1], at.shape)
            for side in (west, east)
            for k in (near, corner)
        ]
        cells = jnp.where(
            at == 0, spread[0], jnp.where(at == 1, spread[1], jnp.where(at == 2, spread[2], spread[3]))
        ).astype(BF16)
        block[index, :16] = cells[:, :LANES]
        block[index, 16:] = cells[:, LANES:]
        copies.append(
            pltpu.make_async_copy(block.at[index], out.at[pl.ds(rows, 32)], sems.at[index])
        )
        copies[-1].start()
    for copy in copies:
        copy.wait()


def corners_of(line, chans):
    rows = 2 * chans
    return jnp.concatenate([line[rows : rows + 16], line[rows + 16 : rows + 32]], 1)


def turned(line, flip):
    shape = (LANES, LANES)
    a, b = (iota(shape, 0), iota(shape, 1))
    turn = one_hot(b == a + flip * (LANES - 1 - 2 * a))
    return dot(line, turn)


def shifted(out, centre, top, bottom, west, east, swap_top=None, swap_bottom=None):
    chans = centre.shape[0]
    k, lane = (iota((16, PADDED), 0), iota((16, PADDED), 1))
    placed_west = lax.dot_general(
        west, one_hot(lane == k * LANES), TN, preferred_element_type=F32
    )
    placed_east = lax.dot_general(
        east, one_hot(lane == k * LANES + LANES - 1), TN, preferred_element_type=F32
    )
    lane_in = iota((chans, LANES), 1)
    for block in range(ROWS + 2):
        span = slice(block * LANES, (block + 1) * LANES)
        if block == 0:
            line = top
        elif block == ROWS + 1:
            line = bottom
        else:
            line = centre[:, (block - 1) * LANES : block * LANES].astype(F32)
        left = jnp.where(lane_in == 0, placed_west[:, span], pltpu.roll(line, 1, 1))
        right = jnp.where(lane_in == LANES - 1, placed_east[:, span], pltpu.roll(line, LANES - 1, 1))
        swap = swap_top if block == 0 else swap_bottom if block == ROWS + 1 else None
        if swap is not None:
            left, right = (jnp.where(swap, right, left), jnp.where(swap, left, right))
        out[0, :, span] = left.astype(BF16)
        out[1, :, span] = line.astype(BF16)
        out[2, :, span] = right.astype(BF16)


def lines(top, mid, bottom):
    return jnp.concatenate([top, mid, bottom, jnp.zeros((6, mid.shape[1]), F32)], 0).astype(BF16)


def pad_forward(out, centre, flags, halo):
    from_w, from_e, from_n, from_s = halo
    chans = centre.shape[0]
    upper, lower = (flags[0] == 1, flags[1] == 1)
    above, below = (corners_of(ref, chans).astype(F32) for ref in (from_n, from_s))
    nw, ne, sw, se = (above[:1], above[2:3], below[:1], below[2:3])
    west = lines(jnp.where(upper, ne, nw), from_w[...].astype(F32)[:ROWS], jnp.where(lower, se, sw))
    east = lines(jnp.where(upper, nw, ne), from_e[...].astype(F32)[:ROWS], jnp.where(lower, sw, se))
    top = turned(from_n[:chans], flags[0])
    bottom = turned(from_s[:chans], flags[1])
    shifted(out, centre, top, bottom, west, east)


def pad_backward(out, centre, flags, halo):
    from_w, from_e, from_n, from_s = halo
    chans = centre.shape[0]
    upper, lower = (flags[0] == 1, flags[1] == 1)
    none = jnp.zeros((1, chans), F32)
    west = lines(none, from_w[...].astype(F32)[ROWS : 2 * ROWS], none)
    east = lines(none, from_e[...].astype(F32)[ROWS : 2 * ROWS], none)
    top = turned(from_n[chans : 2 * chans], flags[0])
    bottom = turned(from_s[chans : 2 * chans], flags[1])
    shifted(out, centre, top, bottom, west, east, upper, lower)


def conv(weight, pads):
    total = None
    for tap in range(9):
        r, s = divmod(tap, 3)
        term = dot(weight[tap], pads[s, :, r * LANES : r * LANES + CELLS])
        total = term if total is None else total + term
    return total


def conv_adjoint(weight, pads, flags, halo):
    total = None
    for tap in range(9):
        r, s = divmod(tap, 3)
        start = (2 - r) * LANES
        term = lax.dot_general(
            weight[tap], pads[2 - s, :, start : start + CELLS], TN, preferred_element_type=F32
        )
        total = term if total is None else total + term
    chans = total.shape[0]
    above, below = (corners_of(ref, chans) for ref in halo[2:])
    k, lane = (iota((16, LANES), 0), iota((16, LANES), 1))

    def corner(block, which, at, tap):
        spread = lax.dot_general(
            block, one_hot((k == which) & (lane == at)), TN, preferred_element_type=F32
        ).astype(BF16)
        return lax.dot_general(weight[tap], spread, TN, preferred_element_type=F32)

    east = LANES - 1
    top = corner(above, 1, 0, 8 - 2 * flags[2]) + corner(above, 3, east, 6 + 2 * flags[3])
    bottom = corner(below, 1, 0, 2 - 2 * flags[4]) + corner(below, 3, east, 2 * flags[5])
    return jnp.concatenate(
        [total[:, :LANES] + top, total[:, LANES : CELLS - LANES], total[:, CELLS - LANES :] + bottom],
        1,
    )


def prepare_kernel(flips, field, cotangent, *outs):
    flat_field, flat_cot = outs[:2]
    for row in range(ROWS):
        span = slice(row * LANES, (row + 1) * LANES)
        flat_field[:, span] = field[:, row, :]
        flat_cot[:, span] = cotangent[:, row, :]
    rims(flat_field[...], flat_cot[...], edge_flags(flips), outs[2:])


def hidden_kernel(flips, field, cotangent, one, two, *refs):
    halo, outs, back_pads = (refs[:4], refs[4:-1], refs[-1])
    act_out, back_out, pads = outs[:3]
    flags = edge_flags(flips)
    pad_forward(pads, field[...], flags, halo)
    pad_backward(back_pads, cotangent[...], flags, halo)
    hidden = conv(one, pads)
    back_act = conv_adjoint(two, back_pads, flags, halo)
    sigma = 1.0 / (1.0 + jnp.exp(-hidden))
    act_out[...] = (hidden * sigma).astype(BF16)
    back_out[...] = (back_act * sigma * (1.0 + hidden * (1.0 - sigma))).astype(BF16)
    rims(act_out[...], back_out[...], flags, outs[3:])


def grad_kernel(grad_tile, pads, keep, away, both):
    core = lax.rem(lax.axis_index("dp"), 2)
    for tap in range(9):
        r, s = divmod(tap, 3)
        term = lax.dot_general(
            grad_tile[...], pads[s, :, r * LANES : r * LANES + CELLS], NT, preferred_element_type=F32
        )
        chans = term.shape[0]
        for part in range(2):
            half, group = divmod(2 * tap + part, 9)
            place = core if half == 0 else 1 - core
            both[place, group * chans : (group + 1) * chans] = term[:, part * LANES : (part + 1) * LANES]
    keep[...] = both[0]
    away[...] = both[1].astype(BF16)


def grad_two_kernel(flips, act, cotangent, *refs):
    halo, pads, outs = (refs[:4], refs[4], refs[5:])
    pad_forward(pads, act[...], edge_flags(flips), halo)
    grad_kernel(cotangent, pads, *outs)


def output_kernel(field, weight, pads, output):
    total = (field[...].astype(F32) + conv(weight, pads)).astype(BF16)
    for row in range(ROWS):
        output[:, row, :] = total[:, row * LANES : (row + 1) * LANES]


def grad_fields_kernel(flips, cotangent, back, weight, *refs):
    halo, (grad_fields, back_pads) = (refs[:4], refs[4:])
    flags = edge_flags(flips)
    pad_backward(back_pads, back[...], flags, halo)
    total = (cotangent[...].astype(F32) + conv_adjoint(weight, back_pads, flags, halo)).astype(BF16)
    for row in range(ROWS):
        grad_fields[:, row, :] = total[:, row * LANES : (row + 1) * LANES]


def finish_kernel(own, near, far, *refs):
    outs, (flat, stage, sems) = (refs[-5:-3], refs[-3:])
    place = lax.axis_index("dp")
    side, core = (lax.shift_right_logical(place, 1), lax.rem(place, 2))
    half = core if own else 1 - core
    chans = stage.shape[2]
    tiles, depth = near.shape[:2]
    depth = depth // 2
    size = tiles * depth
    for which in range(2):
        for tile in range(tiles):
            rows = slice(which * depth, (which + 1) * depth)
            for ref, to in ((near, side), (far, 1 - side)):
                start = pl.multiple_of(to * size + tile * depth, 16)
                flat[which, pl.ds(start, depth)] = ref[tile, rows, :]

    def place_half(odd):
        copies = []
        for which, out in enumerate(outs):
            for slot in range(5):
                lanes = slice(0, 2 * LANES)
                for part in range(2):
                    group = 2 * slot + part - odd
                    if 0 <= group < 9:
                        span = slice(part * LANES, (part + 1) * LANES)
                        rows = slice(group * chans, (group + 1) * chans)
                        stage[which, slot, :, span] = flat[which, rows].astype(F32)
                    else:
                        lanes = slice((1 - part) * LANES, (2 - part) * LANES)
                copies.append(
                    pltpu.make_async_copy(
                        stage.at[which, slot, :, lanes],
                        out.at[slot + 4 * odd, :, lanes],
                        sems.at[which, slot],
                    )
                )
                copies[-1].start()
        for copy in copies:
            copy.wait()

    @pl.when(half == 0)
    def _():
        place_half(0)

    @pl.when(half == 1)
    def _():
        place_half(1)


def finish(own, near, far, *partial):
    chans = partial[0].shape[1] if partial else 2 * LANES
    grad = struct(9, chans, chans, dtype=F32)
    return pl.pallas_call(
        functools.partial(finish_kernel, own),
        out_shape=(grad, grad),
        in_specs=[VMEM, VMEM] + [ANY] * len(partial),
        out_specs=(ANY, ANY),
        input_output_aliases={2 + k: k for k in range(len(partial))},
        scratch_shapes=[
            pltpu.VMEM((2, 9 * chans, LANES), BF16),
            pltpu.VMEM((2, 5, chans, chans), F32),
            pltpu.SemaphoreType.DMA((2, 5)),
        ],
        compiler_params=pltpu.CompilerParams(vmem_limit_bytes=56 * 1024 * 1024),
    )(near, far, *partial)


SMEM = pl.BlockSpec(memory_space=pltpu.SMEM)
VMEM = pl.BlockSpec(memory_space=pltpu.VMEM)
ANY = pl.BlockSpec(memory_space=pl.ANY)


def call(kernel, out_shape, args, scratch=(), flags=True):
    return pl.pallas_call(
        kernel,
        out_shape=out_shape,
        in_specs=([SMEM] if flags else []) + [VMEM] * (len(args) - (1 if flags else 0)),
        out_specs=jax.tree.map(lambda _: VMEM, out_shape),
        scratch_shapes=list(scratch),
        compiler_params=pltpu.CompilerParams(vmem_limit_bytes=56 * 1024 * 1024),
    )(*args)


def struct(*shape, dtype=BF16):
    return jax.ShapeDtypeStruct(shape, dtype)


def rim_shapes(chans):
    side = struct(4 * ROWS, chans)
    line = struct(2 * chans + 32, LANES)
    return (side, side, line, line)


def exchange(rim):
    east, west, south, north = rim
    lons, lats = (lax.axis_size("lon"), lax.axis_size("lat"))

    def along(value, step):
        return lax.ppermute(value, "lon", [(i, (i + step) % lons) for i in range(lons)])

    def across(value, step):
        return lax.ppermute(
            value, "lat", [(i, i + step) for i in range(lats) if 0 <= i + step < lats]
        )

    from_w, from_e = (along(east, 1), along(west, -1))
    line = struct(*south.shape)
    south, north = pl.pallas_call(
        join_kernel,
        name="join",
        out_shape=(line, line),
        in_specs=[ANY, ANY, VMEM, VMEM],
        out_specs=(ANY, ANY),
        input_output_aliases={0: 0, 1: 1},
        scratch_shapes=[pltpu.VMEM((2, 32, LANES), BF16), pltpu.SemaphoreType.DMA((2,))],
    )(south, north, from_w, from_e)
    from_n = across(south, 1)
    from_s = across(north, -1)
    return (from_w, from_e, from_n, from_s)


def beside(value):
    return lax.ppermute(value, "dp", [(i, (i + 2) % 4) for i in range(4)])


def paired(value):
    return lax.ppermute(value, "dp", [(0, 1), (1, 0), (2, 3), (3, 2)])


def over(value, axis):
    return lax.all_to_all(value, axis, 0, 0)


def total(parts):
    return jnp.sum(parts.astype(F32), 0)


def fold(grad):
    keep, away = grad
    got = paired(away)
    side = lax.shift_right_logical(lax.axis_index("dp"), 1)
    half = keep.shape[0] // 2

    def rows(which):
        pick = lambda value: lax.dynamic_slice_in_dim(value, which * half, half, 0).astype(F32)
        return pick(keep) + pick(got)

    return (rows(side), beside(rows(1 - side).astype(BF16)))


def gathered(value, axis):
    return over(jnp.broadcast_to(value[None], (lax.axis_size(axis),) + value.shape), axis)


def reduce_grads(one, two):
    lats, lons = (lax.axis_size("lat"), lax.axis_size("lon"))
    parts = [
        (kept + got.astype(F32)).astype(BF16).reshape(lats, -1, LANES) for kept, got in (one, two)
    ]
    share = total(over(jnp.concatenate(parts, 1), "lat"))
    share = total(over(share.reshape(lons, share.shape[0] // lons, LANES), "lon")).astype(BF16)
    share = gathered(share, "lon")
    return gathered(share.reshape(-1, LANES), "lat")


def per_device(fields, weight_one, weight_two, edge_flips, cotangent):
    chans = fields.shape[1]
    tile = struct(chans, ROWS, LANES)
    flat = struct(chans, CELLS)
    pads = struct(3, chans, PADDED)
    scratch = [pltpu.VMEM((3, chans, PADDED), BF16)]
    field, cot, *rim = call(
        prepare_kernel,
        (flat, flat) + rim_shapes(chans),
        (edge_flips, fields.reshape(tile.shape), cotangent.reshape(tile.shape)),
    )
    halo = exchange(rim)
    act, back, pads_in, *rim = call(
        hidden_kernel,
        (flat, flat, pads) + rim_shapes(chans),
        (edge_flips, field, cot, weight_one, weight_two) + halo,
        scratch,
    )
    halo = exchange(rim)
    local = (struct(9 * chans, LANES, dtype=F32), struct(9 * chans, LANES))
    halves = [pltpu.VMEM((2, 9 * chans, LANES), F32)]
    one = call(grad_kernel, local, (back, pads_in), halves, flags=False)
    one = fold(one)
    pads_act, *two = call(grad_two_kernel, (pads,) + local, (edge_flips, act, cot) + halo, halves)
    two = fold(two)
    output = call(output_kernel, tile, (field, weight_two, pads_act), flags=False)
    quarter = reduce_grads(one, two)
    other = beside(quarter)
    grad_fields = call(
        grad_fields_kernel, tile, (edge_flips, cot, back, weight_one) + halo, scratch
    )
    pair = paired(quarter)
    across = paired(other)
    grads = finish(True, quarter, other)
    grad_one, grad_two = finish(False, pair, across, *grads)
    return (output.reshape(fields.shape), grad_fields.reshape(fields.shape), grad_one, grad_two)


def solution(mesh):
    in_specs = (P("dp", None, "lat", "lon"), P(), P(), P(), P("dp", None, "lat", "lon"))
    out_specs = (P("dp", None, "lat", "lon"), P("dp", None, "lat", "lon"), P(), P())


    return jax.shard_map(
        per_device, mesh=mesh, in_specs=in_specs, out_specs=out_specs, check_vma=False
    )
```

```python
import functools

import jax
import jax.numpy as jnp
from jax import lax
from jax.experimental import pallas as pl
from jax.experimental.pallas import tpu as pltpu
from jax.sharding import PartitionSpec as P


F32 = jnp.float32
BF16 = jnp.bfloat16
LANES = 128
ROWS = 8
CELLS = ROWS * LANES
PADDED = CELLS + 2 * LANES
NT = (((1,), (1,)), ((), ()))
TN = (((0,), (0,)), ((), ()))


def iota(shape, dim):
    return lax.broadcasted_iota(jnp.int32, shape, dim)


def one_hot(cond):
    return jnp.where(cond, 1.0, 0.0).astype(BF16)


def dot(a, b):
    return jnp.dot(a, b, preferred_element_type=F32)


def edge_flags(flips):
    a, o = (lax.axis_index("lat"), lax.axis_index("lon"))
    edges, lons = flips.shape

    def upper(col):
        return jnp.where(a > 0, flips[jnp.maximum(a - 1, 0), col], 0)

    def lower(col):
        return jnp.where(a < edges, flips[jnp.minimum(a, edges - 1), col], 0)

    west, east = (lax.rem(o + lons - 1, lons), lax.rem(o + 1, lons))
    return (upper(o), lower(o), upper(west), upper(east), lower(west), lower(east))


def rims(first, second, flags, outs):
    east, west, south, north = outs
    shape = (2 * ROWS, CELLS)
    row, cell = (iota(shape, 0), iota(shape, 1))
    pick = one_hot(cell == jnp.where(row < ROWS, row * LANES + LANES - 1, (row - ROWS) * LANES))
    one = lax.dot_general(pick, first, NT, preferred_element_type=F32)
    two = lax.dot_general(pick, second, NT, preferred_element_type=F32)
    chans = first.shape[0]
    upper, lower = (flags[0] == 1, flags[1] == 1)
    end = ROWS - 1

    def side(out, base, far):
        top = jnp.where(upper, two[far : far + 1], two[base : base + 1])
        low = jnp.where(lower, two[far + end : far + ROWS], two[base + end : base + ROWS])
        at = iota((ROWS, chans), 0)
        corners = jnp.where(at == 0, jnp.broadcast_to(top, at.shape), jnp.broadcast_to(low, at.shape))
        out[...] = jnp.concatenate(
            [one[base : base + ROWS], two[base : base + ROWS], corners, corners], 0
        ).astype(BF16)

    side(east, 0, ROWS)
    side(west, ROWS, 0)
    south[:chans] = first[:, CELLS - LANES :]
    south[chans : 2 * chans] = second[:, CELLS - LANES :]
    north[:chans] = first[:, :LANES]
    north[chans : 2 * chans] = second[:, :LANES]


def join_kernel(south, north, from_w, from_e, south_out, north_out, block, sems):
    rows = south_out.shape[0] - 32
    west, east = (from_w[...].astype(F32), from_e[...].astype(F32))
    at = iota((16, west.shape[1]), 0)
    copies = []
    for index, (out, near, corner) in enumerate(((south_out, 7, 17), (north_out, 0, 16))):
        spread = [
            jnp.broadcast_to(side[k : k + 1], at.shape)
            for side in (west, east)
            for k in (near, corner)
        ]
        cells = jnp.where(
            at == 0, spread[0], jnp.where(at == 1, spread[1], jnp.where(at == 2, spread[2], spread[3]))
        ).astype(BF16)
        block[index, :16] = cells[:, :LANES]
        block[index, 16:] = cells[:, LANES:]
        copies.append(
            pltpu.make_async_copy(block.at[index], out.at[pl.ds(rows, 32)], sems.at[index])
        )
        copies[-1].start()
    for copy in copies:
        copy.wait()


def corners_of(line, chans):
    rows = 2 * chans
    return jnp.concatenate([line[rows : rows + 16], line[rows + 16 : rows + 32]], 1)


def turned(line, flip):
    shape = (LANES, LANES)
    a, b = (iota(shape, 0), iota(shape, 1))
    turn = one_hot(b == a + flip * (LANES - 1 - 2 * a))
    return dot(line, turn)


def shifted(out, centre, top, bottom, west, east, swaps=(None, None)):
    swap_top, swap_bottom = swaps
    order = (0, 1, 2) if swap_top is None else (2, 1, 0)
    chans = centre.shape[0]
    k, lane = (iota((16, PADDED), 0), iota((16, PADDED), 1))
    placed_west = lax.dot_general(
        west, one_hot(lane == k * LANES), TN, preferred_element_type=F32
    )
    placed_east = lax.dot_general(
        east, one_hot(lane == k * LANES + LANES - 1), TN, preferred_element_type=F32
    )
    lane_in = iota((chans, LANES), 1)
    for block in range(ROWS + 2):
        span = slice(block * LANES, (block + 1) * LANES)
        if block == 0:
            line = top
        elif block == ROWS + 1:
            line = bottom
        else:
            line = centre[:, (block - 1) * LANES : block * LANES].astype(F32)
        left = jnp.where(lane_in == 0, placed_west[:, span], pltpu.roll(line, 1, 1))
        right = jnp.where(lane_in == LANES - 1, placed_east[:, span], pltpu.roll(line, LANES - 1, 1))
        swap = swap_top if block == 0 else swap_bottom if block == ROWS + 1 else None
        if swap is not None:
            left, right = (jnp.where(swap, right, left), jnp.where(swap, left, right))
        for slot, cells in zip(order, (left, line, right)):
            out[slot * chans : (slot + 1) * chans, span] = cells.astype(BF16)


def lines(top, mid, bottom):
    return jnp.concatenate([top, mid, bottom, jnp.zeros((6, mid.shape[1]), F32)], 0).astype(BF16)


def pad_forward(out, centre, flags, halo):
    from_w, from_e, from_n, from_s = halo
    chans = centre.shape[0]
    upper, lower = (flags[0] == 1, flags[1] == 1)
    above, below = (corners_of(ref, chans).astype(F32) for ref in (from_n, from_s))
    nw, ne, sw, se = (above[:1], above[2:3], below[:1], below[2:3])
    west = lines(jnp.where(upper, ne, nw), from_w[...].astype(F32)[:ROWS], jnp.where(lower, se, sw))
    east = lines(jnp.where(upper, nw, ne), from_e[...].astype(F32)[:ROWS], jnp.where(lower, sw, se))
    top = turned(from_n[:chans], flags[0])
    bottom = turned(from_s[:chans], flags[1])
    shifted(out, centre, top, bottom, west, east)


def pad_backward(out, centre, flags, halo):
    from_w, from_e, from_n, from_s = halo
    chans = centre.shape[0]
    upper, lower = (flags[0] == 1, flags[1] == 1)
    none = jnp.zeros((1, chans), F32)
    west = lines(none, from_w[...].astype(F32)[ROWS : 2 * ROWS], none)
    east = lines(none, from_e[...].astype(F32)[ROWS : 2 * ROWS], none)
    top = turned(from_n[chans : 2 * chans], flags[0])
    bottom = turned(from_s[chans : 2 * chans], flags[1])
    shifted(out, centre, top, bottom, west, east, (upper, lower))


def conv(weight, pads):
    total = None
    for r in range(3):
        taps = jnp.concatenate([weight[3 * r + s] for s in range(3)], 1)
        term = dot(taps, pads[:, r * LANES : r * LANES + CELLS])
        total = term if total is None else total + term
    return total


def conv_adjoint(weight, pads, flags, halo):
    total = None
    for r in range(3):
        start = (2 - r) * LANES
        taps = jnp.concatenate([weight[3 * r + s] for s in range(3)], 0)
        term = lax.dot_general(
            taps, pads[:, start : start + CELLS], TN, preferred_element_type=F32
        )
        total = term if total is None else total + term
    chans = total.shape[0]
    above, below = (corners_of(ref, chans) for ref in halo[2:])
    k, lane = (iota((16, LANES), 0), iota((16, LANES), 1))

    def corner(block, which, at, tap):
        spread = lax.dot_general(
            block, one_hot((k == which) & (lane == at)), TN, preferred_element_type=F32
        ).astype(BF16)
        return lax.dot_general(weight[tap], spread, TN, preferred_element_type=F32)

    east = LANES - 1
    top = corner(above, 1, 0, 8 - 2 * flags[2]) + corner(above, 3, east, 6 + 2 * flags[3])
    bottom = corner(below, 1, 0, 2 - 2 * flags[4]) + corner(below, 3, east, 2 * flags[5])
    return jnp.concatenate(
        [total[:, :LANES] + top, total[:, LANES : CELLS - LANES], total[:, CELLS - LANES :] + bottom],
        1,
    )


def prepare_kernel(flips, field, cotangent, *outs):
    flat_field, flat_cot = outs[:2]
    for row in range(ROWS):
        span = slice(row * LANES, (row + 1) * LANES)
        flat_field[:, span] = field[:, row, :]
        flat_cot[:, span] = cotangent[:, row, :]
    rims(flat_field[...], flat_cot[...], edge_flags(flips), outs[2:])


def hidden_kernel(flips, field, cotangent, one, two, *refs):
    halo, outs, back_pads = (refs[:4], refs[4:-1], refs[-1])
    act_out, back_out, pads = outs[:3]
    flags = edge_flags(flips)
    pad_forward(pads, field[...], flags, halo)
    pad_backward(back_pads, cotangent[...], flags, halo)
    hidden = conv(one, pads)
    back_act = conv_adjoint(two, back_pads, flags, halo)
    sigma = 1.0 / (1.0 + jnp.exp(-hidden))
    act_out[...] = (hidden * sigma).astype(BF16)
    back_out[...] = (back_act * sigma * (1.0 + hidden * (1.0 - sigma))).astype(BF16)
    rims(act_out[...], back_out[...], flags, outs[3:])


def grad_kernel(grad_tile, pads, keep, away, both):
    core = lax.rem(lax.axis_index("dp"), 2)
    chans = grad_tile.shape[0]
    for r in range(3):
        terms = lax.dot_general(
            grad_tile[...], pads[:, r * LANES : r * LANES + CELLS], NT, preferred_element_type=F32
        )
        for piece in range(6):
            half, group = divmod(6 * r + piece, 9)
            place = core if half == 0 else 1 - core
            rows = slice(group * chans, (group + 1) * chans)
            both[place, rows] = terms[:, piece * LANES : (piece + 1) * LANES]
    keep[...] = both[0]
    away[...] = both[1].astype(BF16)


def grad_two_kernel(flips, act, cotangent, *refs):
    halo, pads, outs = (refs[:4], refs[4], refs[5:])
    pad_forward(pads, act[...], edge_flags(flips), halo)
    grad_kernel(cotangent, pads, *outs)


def output_kernel(field, weight, pads, output):
    total = (field[...].astype(F32) + conv(weight, pads)).astype(BF16)
    for row in range(ROWS):
        output[:, row, :] = total[:, row * LANES : (row + 1) * LANES]


def grad_fields_kernel(flips, cotangent, back, weight, *refs):
    halo, (grad_fields, back_pads) = (refs[:4], refs[4:])
    flags = edge_flags(flips)
    pad_backward(back_pads, back[...], flags, halo)
    total = (cotangent[...].astype(F32) + conv_adjoint(weight, back_pads, flags, halo)).astype(BF16)
    for row in range(ROWS):
        grad_fields[:, row, :] = total[:, row * LANES : (row + 1) * LANES]


def finish_kernel(own, near, far, *refs):
    outs, (flat, stage, sems, got) = (refs[-6:-4], refs[-4:])
    place = lax.axis_index("dp")
    side, core = (lax.shift_right_logical(place, 1), lax.rem(place, 2))
    half = core if own else 1 - core
    chans = stage.shape[2]
    tiles, depth = near.shape[:2]
    depth = depth // 2
    size = tiles * depth
    loads = []
    for which in range(2):
        for tile in range(tiles):
            for index, (ref, to) in enumerate(((near, side), (far, 1 - side))):
                start = pl.multiple_of(to * size + tile * depth, 16)
                loads.append(
                    pltpu.make_async_copy(
                        ref.at[tile, pl.ds(which * depth, depth), :],
                        flat.at[which, pl.ds(start, depth), :],
                        got.at[which, tile, index],
                    )
                )
                loads[-1].start()
    for load in loads:
        load.wait()

    def place_half(odd):
        copies = []
        for which, out in enumerate(outs):
            for slot in range(5):
                lanes = slice(0, 2 * LANES)
                for part in range(2):
                    group = 2 * slot + part - odd
                    if 0 <= group < 9:
                        span = slice(part * LANES, (part + 1) * LANES)
                        rows = slice(group * chans, (group + 1) * chans)
                        stage[which, slot, :, span] = flat[which, rows].astype(F32)
                    else:
                        lanes = slice((1 - part) * LANES, (2 - part) * LANES)
                copies.append(
                    pltpu.make_async_copy(
                        stage.at[which, slot, :, lanes],
                        out.at[slot + 4 * odd, :, lanes],
                        sems.at[which, slot],
                    )
                )
                copies[-1].start()
        for copy in copies:
            copy.wait()

    @pl.when(half == 0)
    def _():
        place_half(0)

    @pl.when(half == 1)
    def _():
        place_half(1)


def finish(own, near, far, *partial):
    chans = partial[0].shape[1] if partial else 2 * LANES
    grad = struct(9, chans, chans, dtype=F32)
    return pl.pallas_call(
        functools.partial(finish_kernel, own),
        out_shape=(grad, grad),
        in_specs=[ANY, ANY] + [ANY] * len(partial),
        out_specs=(ANY, ANY),
        input_output_aliases={2 + k: k for k in range(len(partial))},
        scratch_shapes=[
            pltpu.VMEM((2, 9 * chans, LANES), BF16),
            pltpu.VMEM((2, 5, chans, chans), F32),
            pltpu.SemaphoreType.DMA((2, 5)),
            pltpu.SemaphoreType.DMA((2, near.shape[0], 2)),
        ],
        compiler_params=pltpu.CompilerParams(vmem_limit_bytes=56 * 1024 * 1024),
    )(near, far, *partial)


SMEM = pl.BlockSpec(memory_space=pltpu.SMEM)
VMEM = pl.BlockSpec(memory_space=pltpu.VMEM)
ANY = pl.BlockSpec(memory_space=pl.ANY)


def call(kernel, out_shape, args, scratch=(), flags=True):
    return pl.pallas_call(
        kernel,
        out_shape=out_shape,
        in_specs=([SMEM] if flags else []) + [VMEM] * (len(args) - (1 if flags else 0)),
        out_specs=jax.tree.map(lambda _: VMEM, out_shape),
        scratch_shapes=list(scratch),
        compiler_params=pltpu.CompilerParams(vmem_limit_bytes=56 * 1024 * 1024),
    )(*args)


def struct(*shape, dtype=BF16):
    return jax.ShapeDtypeStruct(shape, dtype)


def rim_shapes(chans):
    side = struct(4 * ROWS, chans)
    line = struct(2 * chans + 32, LANES)
    return (side, side, line, line)


def exchange(rim):
    east, west, south, north = rim
    lons, lats = (lax.axis_size("lon"), lax.axis_size("lat"))

    def along(value, step):
        return lax.ppermute(value, "lon", [(i, (i + step) % lons) for i in range(lons)])

    def across(value, step):
        return lax.ppermute(
            value, "lat", [(i, i + step) for i in range(lats) if 0 <= i + step < lats]
        )

    from_w, from_e = (along(east, 1), along(west, -1))
    line = struct(*south.shape)
    south, north = pl.pallas_call(
        join_kernel,
        name="join",
        out_shape=(line, line),
        in_specs=[ANY, ANY, VMEM, VMEM],
        out_specs=(ANY, ANY),
        input_output_aliases={0: 0, 1: 1},
        scratch_shapes=[pltpu.VMEM((2, 32, LANES), BF16), pltpu.SemaphoreType.DMA((2,))],
    )(south, north, from_w, from_e)
    from_n = across(south, 1)
    from_s = across(north, -1)
    return (from_w, from_e, from_n, from_s)


def beside(value):
    return lax.ppermute(value, "dp", [(i, (i + 2) % 4) for i in range(4)])


def paired(value):
    return lax.ppermute(value, "dp", [(0, 1), (1, 0), (2, 3), (3, 2)])


def over(value, axis):
    return lax.all_to_all(value, axis, 0, 0)


def total(parts):
    return jnp.sum(parts.astype(F32), 0)


def fold(grad):
    keep, away = grad
    got = paired(away)
    side = lax.shift_right_logical(lax.axis_index("dp"), 1)
    half = keep.shape[0] // 2

    def rows(which):
        pick = lambda value: lax.dynamic_slice_in_dim(value, which * half, half, 0).astype(F32)
        return pick(keep) + pick(got)

    return (rows(side), beside(rows(1 - side).astype(BF16)))


def gathered(value, axis):
    return over(jnp.broadcast_to(value[None], (lax.axis_size(axis),) + value.shape), axis)


def reduce_grads(one, two):
    lats, lons = (lax.axis_size("lat"), lax.axis_size("lon"))
    parts = [
        (kept + got.astype(F32)).astype(BF16).reshape(lats, -1, LANES) for kept, got in (one, two)
    ]
    share = total(over(jnp.concatenate(parts, 1), "lat"))
    share = total(over(share.reshape(lons, share.shape[0] // lons, LANES), "lon")).astype(BF16)
    share = gathered(share, "lon")
    return gathered(share.reshape(-1, LANES), "lat")


def per_device(fields, weight_one, weight_two, edge_flips, cotangent):
    chans = fields.shape[1]
    tile = struct(chans, ROWS, LANES)
    flat = struct(chans, CELLS)
    pads = struct(3 * chans, PADDED)
    scratch = [pltpu.VMEM((3 * chans, PADDED), BF16)]
    field, cot, *rim = call(
        prepare_kernel,
        (flat, flat) + rim_shapes(chans),
        (edge_flips, fields.reshape(tile.shape), cotangent.reshape(tile.shape)),
    )
    halo = exchange(rim)
    act, back, pads_in, *rim = call(
        hidden_kernel,
        (flat, flat, pads) + rim_shapes(chans),
        (edge_flips, field, cot, weight_one, weight_two) + halo,
        scratch,
    )
    halo = exchange(rim)
    local = (struct(9 * chans, LANES, dtype=F32), struct(9 * chans, LANES))
    halves = [pltpu.VMEM((2, 9 * chans, LANES), F32)]
    one = call(grad_kernel, local, (back, pads_in), halves, flags=False)
    one = fold(one)
    pads_act, *two = call(grad_two_kernel, (pads,) + local, (edge_flips, act, cot) + halo, halves)
    two = fold(two)
    output = call(output_kernel, tile, (field, weight_two, pads_act), flags=False)
    quarter = reduce_grads(one, two)
    other = beside(quarter)
    grad_fields = call(
        grad_fields_kernel, tile, (edge_flips, cot, back, weight_one) + halo, scratch
    )
    pair = paired(quarter)
    across = paired(other)
    grads = finish(True, quarter, other)
    grad_one, grad_two = finish(False, pair, across, *grads)
    return (output.reshape(fields.shape), grad_fields.reshape(fields.shape), grad_one, grad_two)


def solution(mesh):
    in_specs = (P("dp", None, "lat", "lon"), P(), P(), P(), P("dp", None, "lat", "lon"))
    out_specs = (P("dp", None, "lat", "lon"), P("dp", None, "lat", "lon"), P(), P())


    return jax.shard_map(
        per_device, mesh=mesh, in_specs=in_specs, out_specs=out_specs, check_vma=False
    )
```

```python
import functools

import jax
import jax.numpy as jnp
from jax import lax
from jax.experimental import pallas as pl
from jax.experimental.pallas import tpu as pltpu
from jax.sharding import PartitionSpec as P


F32 = jnp.float32
BF16 = jnp.bfloat16
LANES = 128
ROWS = 8
CELLS = ROWS * LANES
PADDED = CELLS + 2 * LANES
NT = (((1,), (1,)), ((), ()))
TN = (((0,), (0,)), ((), ()))


def iota(shape, dim):
    return lax.broadcasted_iota(jnp.int32, shape, dim)


def one_hot(cond):
    return jnp.where(cond, 1.0, 0.0).astype(BF16)


def dot(a, b):
    return jnp.dot(a, b, preferred_element_type=F32)


def edge_flags(flips):
    a, o = (lax.axis_index("lat"), lax.axis_index("lon"))
    edges, lons = flips.shape

    def upper(col):
        return jnp.where(a > 0, flips[jnp.maximum(a - 1, 0), col], 0)

    def lower(col):
        return jnp.where(a < edges, flips[jnp.minimum(a, edges - 1), col], 0)

    west, east = (lax.rem(o + lons - 1, lons), lax.rem(o + 1, lons))
    return (upper(o), lower(o), upper(west), upper(east), lower(west), lower(east))


def rims(first, second, flags, outs):
    east, west, south, north = outs
    shape = (2 * ROWS, CELLS)
    row, cell = (iota(shape, 0), iota(shape, 1))
    pick = one_hot(cell == jnp.where(row < ROWS, row * LANES + LANES - 1, (row - ROWS) * LANES))
    one = lax.dot_general(pick, first, NT, preferred_element_type=F32)
    two = lax.dot_general(pick, second, NT, preferred_element_type=F32)
    chans = first.shape[0]
    upper, lower = (flags[0] == 1, flags[1] == 1)
    end = ROWS - 1

    def side(out, base, far):
        top = jnp.where(upper, two[far : far + 1], two[base : base + 1])
        low = jnp.where(lower, two[far + end : far + ROWS], two[base + end : base + ROWS])
        at = iota((ROWS, chans), 0)
        corners = jnp.where(at == 0, jnp.broadcast_to(top, at.shape), jnp.broadcast_to(low, at.shape))
        out[...] = jnp.concatenate(
            [one[base : base + ROWS], two[base : base + ROWS], corners, corners], 0
        ).astype(BF16)

    side(east, 0, ROWS)
    side(west, ROWS, 0)
    south[:chans] = first[:, CELLS - LANES :]
    south[chans : 2 * chans] = second[:, CELLS - LANES :]
    north[:chans] = first[:, :LANES]
    north[chans : 2 * chans] = second[:, :LANES]


def join_kernel(south, north, from_w, from_e, south_out, north_out, block, sems):
    rows = south_out.shape[0] - 32
    west, east = (from_w[...].astype(F32), from_e[...].astype(F32))
    at = iota((16, west.shape[1]), 0)
    copies = []
    for index, (out, near, corner) in enumerate(((south_out, 7, 17), (north_out, 0, 16))):
        spread = [
            jnp.broadcast_to(side[k : k + 1], at.shape)
            for side in (west, east)
            for k in (near, corner)
        ]
        cells = jnp.where(
            at == 0, spread[0], jnp.where(at == 1, spread[1], jnp.where(at == 2, spread[2], spread[3]))
        ).astype(BF16)
        block[index, :16] = cells[:, :LANES]
        block[index, 16:] = cells[:, LANES:]
        copies.append(
            pltpu.make_async_copy(block.at[index], out.at[pl.ds(rows, 32)], sems.at[index])
        )
        copies[-1].start()
    for copy in copies:
        copy.wait()


def corners_of(line, chans):
    rows = 2 * chans
    return jnp.concatenate([line[rows : rows + 16], line[rows + 16 : rows + 32]], 1)


def turned(line, flip):
    shape = (LANES, LANES)
    a, b = (iota(shape, 0), iota(shape, 1))
    turn = one_hot(b == a + flip * (LANES - 1 - 2 * a))
    return dot(line, turn)


def shifted(out, centre, top, bottom, west, east, swaps=(None, None), edges=False):
    swap_top, swap_bottom = swaps
    chans = west.shape[1]
    order = (0, 1, 2) if swap_top is None else (2, 1, 0)
    k, lane = (iota((16, PADDED), 0), iota((16, PADDED), 1))
    placed_west = lax.dot_general(
        west, one_hot(lane == k * LANES), TN, preferred_element_type=F32
    )
    placed_east = lax.dot_general(
        east, one_hot(lane == k * LANES + LANES - 1), TN, preferred_element_type=F32
    )
    lane_in = iota((chans, LANES), 1)
    for block in (0, ROWS + 1) if edges else range(ROWS + 2):
        span = slice(block * LANES, (block + 1) * LANES)
        to = slice(LANES, 2 * LANES) if edges and block else span
        if top is None and block in (0, ROWS + 1):
            out[:, span] = jnp.zeros((3 * chans, LANES), BF16)
            continue
        if block == 0:
            line = top
        elif block == ROWS + 1:
            line = bottom
        else:
            line = centre[:, (block - 1) * LANES : block * LANES].astype(F32)
        left = jnp.where(lane_in == 0, placed_west[:, span], pltpu.roll(line, 1, 1))
        right = jnp.where(lane_in == LANES - 1, placed_east[:, span], pltpu.roll(line, LANES - 1, 1))
        swap = swap_top if block == 0 else swap_bottom if block == ROWS + 1 else None
        if swap is not None:
            left, right = (jnp.where(swap, right, left), jnp.where(swap, left, right))
        for slot, cells in zip(order, (left, line, right)):
            out[slot * chans : (slot + 1) * chans, to] = cells.astype(BF16)


def lines(top, mid, bottom):
    return jnp.concatenate([top, mid, bottom, jnp.zeros((6, mid.shape[1]), F32)], 0).astype(BF16)


def pad_forward(out, centre, flags, halo, part=None):
    from_w, from_e, from_n, from_s = halo
    chans = out.shape[0] // 3
    sides = [jnp.zeros((ROWS, chans), F32)] * 2
    if part != "edges":
        sides = [ref[...].astype(F32)[:ROWS] for ref in (from_w, from_e)]
    if part == "inner":
        none = jnp.zeros((1, chans), F32)
        west, east = (lines(none, side, none) for side in sides)
        shifted(out, centre, None, None, west, east)
        return
    upper, lower = (flags[0] == 1, flags[1] == 1)
    above, below = (corners_of(ref, chans).astype(F32) for ref in (from_n, from_s))
    nw, ne, sw, se = (above[:1], above[2:3], below[:1], below[2:3])
    west = lines(jnp.where(upper, ne, nw), sides[0], jnp.where(lower, se, sw))
    east = lines(jnp.where(upper, nw, ne), sides[1], jnp.where(lower, sw, se))
    top = turned(from_n[:chans], flags[0])
    bottom = turned(from_s[:chans], flags[1])
    shifted(out, centre, top, bottom, west, east, edges=part == "edges")


def pad_backward(out, centre, flags, halo, part=None):
    from_w, from_e, from_n, from_s = halo
    chans = out.shape[0] // 3
    none = jnp.zeros((1, chans), F32)
    sides = [jnp.zeros((ROWS, chans), F32)] * 2
    if part != "edges":
        sides = [ref[...].astype(F32)[ROWS : 2 * ROWS] for ref in (from_w, from_e)]
    west, east = (lines(none, side, none) for side in sides)
    if part == "inner":
        shifted(out, centre, None, None, west, east, (False, False))
        return
    upper, lower = (flags[0] == 1, flags[1] == 1)
    top = turned(from_n[chans : 2 * chans], flags[0])
    bottom = turned(from_s[chans : 2 * chans], flags[1])
    shifted(out, centre, top, bottom, west, east, (upper, lower), part == "edges")


def conv(weight, pads):
    total = None
    for r in range(3):
        taps = jnp.concatenate([weight[3 * r + s] for s in range(3)], 1)
        term = dot(taps, pads[:, r * LANES : r * LANES + CELLS])
        total = term if total is None else total + term
    return total


def adjoint_rows(weight, r, cells):
    taps = jnp.concatenate([weight[3 * r + s] for s in range(3)], 0)
    return lax.dot_general(taps, cells, TN, preferred_element_type=F32)


def adjoint_corners(weight, flags, halo, chans):
    above, below = (corners_of(ref, chans) for ref in halo[2:])
    k, lane = (iota((16, LANES), 0), iota((16, LANES), 1))

    def corner(block, which, at, tap):
        spread = lax.dot_general(
            block, one_hot((k == which) & (lane == at)), TN, preferred_element_type=F32
        ).astype(BF16)
        return lax.dot_general(weight[tap], spread, TN, preferred_element_type=F32)

    east = LANES - 1
    top = corner(above, 1, 0, 8 - 2 * flags[2]) + corner(above, 3, east, 6 + 2 * flags[3])
    bottom = corner(below, 1, 0, 2 - 2 * flags[4]) + corner(below, 3, east, 2 * flags[5])
    return (top, bottom)


def with_ends(total, top, bottom):
    return jnp.concatenate(
        [total[:, :LANES] + top, total[:, LANES : CELLS - LANES], total[:, CELLS - LANES :] + bottom],
        1,
    )


def adjoint_inner(weight, pads):
    total = None
    for r in range(3):
        start = (2 - r) * LANES
        term = adjoint_rows(weight, r, pads[:, start : start + CELLS])
        total = term if total is None else total + term
    return total


def conv_adjoint(weight, pads, flags, halo):
    total = adjoint_inner(weight, pads)
    return with_ends(total, *adjoint_corners(weight, flags, halo, total.shape[0]))


def prepare_kernel(flips, field, cotangent, *outs):
    flat_field, flat_cot = outs[:2]
    for row in range(ROWS):
        span = slice(row * LANES, (row + 1) * LANES)
        flat_field[:, span] = field[:, row, :]
        flat_cot[:, span] = cotangent[:, row, :]
    rims(flat_field[...], flat_cot[...], edge_flags(flips), outs[2:])


def inner_kernel(field, cotangent, one, two, from_w, from_e, pads, hidden, back_act, back_pads):
    halo = (from_w, from_e, None, None)
    pad_forward(pads, field[...], None, halo, "inner")
    hidden[...] = conv(one, pads)
    pad_backward(back_pads, cotangent[...], None, halo, "inner")
    back_act[...] = adjoint_inner(two, back_pads)


def hidden_kernel(flips, pads_in, hidden_in, back_in, one, two, from_n, from_s, *refs):
    act_out, back_out, pads_out = refs[:3]
    ends, back_ends, sems = refs[-3:]
    flags = edge_flags(flips)
    halo = (None, None, from_n, from_s)
    chans = hidden_in.shape[0]
    pad_forward(ends, None, flags, halo, "edges")
    copies = [
        pltpu.make_async_copy(
            ends.at[:, pl.ds(k * LANES, LANES)],
            pads_out.at[:, pl.ds(k * (PADDED - LANES), LANES)],
            sems.at[k],
        )
        for k in range(2)
    ]
    for copy in copies:
        copy.start()
    pad_backward(back_ends, None, flags, halo, "edges")
    first, last = (jnp.concatenate([one[k + s] for s in range(3)], 1) for k in (0, 6))
    hidden = with_ends(
        hidden_in[...], dot(first, ends[:, :LANES]), dot(last, ends[:, LANES:])
    )
    top, bottom = adjoint_corners(two, flags, halo, chans)
    back_act = with_ends(
        back_in[...],
        top + adjoint_rows(two, 2, back_ends[:, :LANES]),
        bottom + adjoint_rows(two, 0, back_ends[:, LANES:]),
    )
    sigma = 1.0 / (1.0 + jnp.exp(-hidden))
    act_out[...] = (hidden * sigma).astype(BF16)
    back_out[...] = (back_act * sigma * (1.0 + hidden * (1.0 - sigma))).astype(BF16)
    rims(act_out[...], back_out[...], flags, refs[3:-3])
    for copy in copies:
        copy.wait()


def grad_kernel(grad_tile, pads, keep, away, both):
    core = lax.rem(lax.axis_index("dp"), 2)
    chans = grad_tile.shape[0]
    for r in range(3):
        terms = lax.dot_general(
            grad_tile[...], pads[:, r * LANES : r * LANES + CELLS], NT, preferred_element_type=F32
        )
        for piece in range(6):
            half, group = divmod(6 * r + piece, 9)
            place = core if half == 0 else 1 - core
            rows = slice(group * chans, (group + 1) * chans)
            both[place, rows] = terms[:, piece * LANES : (piece + 1) * LANES]
    keep[...] = both[0]
    away[...] = both[1].astype(BF16)


def grad_two_kernel(flips, act, cotangent, *refs):
    halo, pads, outs = (refs[:4], refs[4], refs[5:])
    pad_forward(pads, act[...], edge_flags(flips), halo)
    grad_kernel(cotangent, pads, *outs)


def output_kernel(field, weight, pads, output):
    total = (field[...].astype(F32) + conv(weight, pads)).astype(BF16)
    for row in range(ROWS):
        output[:, row, :] = total[:, row * LANES : (row + 1) * LANES]


def grad_fields_kernel(flips, cotangent, back, weight, *refs):
    halo, (grad_fields, back_pads) = (refs[:4], refs[4:])
    flags = edge_flags(flips)
    pad_backward(back_pads, back[...], flags, halo)
    total = (cotangent[...].astype(F32) + conv_adjoint(weight, back_pads, flags, halo)).astype(BF16)
    for row in range(ROWS):
        grad_fields[:, row, :] = total[:, row * LANES : (row + 1) * LANES]


def finish_kernel(own, near, far, *refs):
    outs, (flat, stage, sems, got) = (refs[-6:-4], refs[-4:])
    place = lax.axis_index("dp")
    side, core = (lax.shift_right_logical(place, 1), lax.rem(place, 2))
    half = core if own else 1 - core
    chans = stage.shape[2]
    tiles, depth = near.shape[:2]
    depth = depth // 2
    size = tiles * depth
    loads = []
    for which in range(2):
        for tile in range(tiles):
            for index, (ref, to) in enumerate(((near, side), (far, 1 - side))):
                start = pl.multiple_of(to * size + tile * depth, 16)
                loads.append(
                    pltpu.make_async_copy(
                        ref.at[tile, pl.ds(which * depth, depth), :],
                        flat.at[which, pl.ds(start, depth), :],
                        got.at[which, tile, index],
                    )
                )
                loads[-1].start()
    for load in loads:
        load.wait()

    def place_half(odd):
        copies = []
        for which, out in enumerate(outs):
            for slot in range(5):
                lanes = slice(0, 2 * LANES)
                for part in range(2):
                    group = 2 * slot + part - odd
                    if 0 <= group < 9:
                        span = slice(part * LANES, (part + 1) * LANES)
                        rows = slice(group * chans, (group + 1) * chans)
                        stage[which, slot, :, span] = flat[which, rows].astype(F32)
                    else:
                        lanes = slice((1 - part) * LANES, (2 - part) * LANES)
                copies.append(
                    pltpu.make_async_copy(
                        stage.at[which, slot, :, lanes],
                        out.at[slot + 4 * odd, :, lanes],
                        sems.at[which, slot],
                    )
                )
                copies[-1].start()
        for copy in copies:
            copy.wait()

    @pl.when(half == 0)
    def _():
        place_half(0)

    @pl.when(half == 1)
    def _():
        place_half(1)


def finish(own, near, far, *partial):
    chans = partial[0].shape[1] if partial else 2 * LANES
    grad = struct(9, chans, chans, dtype=F32)
    return pl.pallas_call(
        functools.partial(finish_kernel, own),
        out_shape=(grad, grad),
        in_specs=[ANY, ANY] + [ANY] * len(partial),
        out_specs=(ANY, ANY),
        input_output_aliases={2 + k: k for k in range(len(partial))},
        scratch_shapes=[
            pltpu.VMEM((2, 9 * chans, LANES), BF16),
            pltpu.VMEM((2, 5, chans, chans), F32),
            pltpu.SemaphoreType.DMA((2, 5)),
            pltpu.SemaphoreType.DMA((2, near.shape[0], 2)),
        ],
        compiler_params=pltpu.CompilerParams(vmem_limit_bytes=56 * 1024 * 1024),
    )(near, far, *partial)


SMEM = pl.BlockSpec(memory_space=pltpu.SMEM)
VMEM = pl.BlockSpec(memory_space=pltpu.VMEM)
ANY = pl.BlockSpec(memory_space=pl.ANY)


def call(kernel, out_shape, args, scratch=(), flags=True):
    return pl.pallas_call(
        kernel,
        out_shape=out_shape,
        in_specs=([SMEM] if flags else []) + [VMEM] * (len(args) - (1 if flags else 0)),
        out_specs=jax.tree.map(lambda _: VMEM, out_shape),
        scratch_shapes=list(scratch),
        compiler_params=pltpu.CompilerParams(vmem_limit_bytes=56 * 1024 * 1024),
    )(*args)


def struct(*shape, dtype=BF16):
    return jax.ShapeDtypeStruct(shape, dtype)


def rim_shapes(chans):
    side = struct(4 * ROWS, chans)
    line = struct(2 * chans + 32, LANES)
    return (side, side, line, line)


def exchange(rim):
    east, west, south, north = rim
    lons, lats = (lax.axis_size("lon"), lax.axis_size("lat"))

    def along(value, step):
        return lax.ppermute(value, "lon", [(i, (i + step) % lons) for i in range(lons)])

    def across(value, step):
        return lax.ppermute(
            value, "lat", [(i, i + step) for i in range(lats) if 0 <= i + step < lats]
        )

    from_w, from_e = (along(east, 1), along(west, -1))
    line = struct(*south.shape)
    south, north = pl.pallas_call(
        join_kernel,
        name="join",
        out_shape=(line, line),
        in_specs=[ANY, ANY, VMEM, VMEM],
        out_specs=(ANY, ANY),
        input_output_aliases={0: 0, 1: 1},
        scratch_shapes=[pltpu.VMEM((2, 32, LANES), BF16), pltpu.SemaphoreType.DMA((2,))],
    )(south, north, from_w, from_e)
    from_n = across(south, 1)
    from_s = across(north, -1)
    return (from_w, from_e, from_n, from_s)


def beside(value):
    return lax.ppermute(value, "dp", [(i, (i + 2) % 4) for i in range(4)])


def paired(value):
    return lax.ppermute(value, "dp", [(0, 1), (1, 0), (2, 3), (3, 2)])


def over(value, axis):
    return lax.all_to_all(value, axis, 0, 0)


def total(parts):
    return jnp.sum(parts.astype(F32), 0)


def fold(grad):
    keep, away = grad
    got = paired(away)
    side = lax.shift_right_logical(lax.axis_index("dp"), 1)
    half = keep.shape[0] // 2

    def rows(which):
        pick = lambda value: lax.dynamic_slice_in_dim(value, which * half, half, 0).astype(F32)
        return pick(keep) + pick(got)

    return (rows(side), beside(rows(1 - side).astype(BF16)))


def gathered(value, axis):
    return over(jnp.broadcast_to(value[None], (lax.axis_size(axis),) + value.shape), axis)


def reduce_grads(one, two):
    lats, lons = (lax.axis_size("lat"), lax.axis_size("lon"))
    parts = [
        (kept + got.astype(F32)).astype(BF16).reshape(lats, -1, LANES) for kept, got in (one, two)
    ]
    share = total(over(jnp.concatenate(parts, 1), "lat"))
    share = total(over(share.reshape(lons, share.shape[0] // lons, LANES), "lon")).astype(BF16)
    share = gathered(share, "lon")
    return gathered(share.reshape(-1, LANES), "lat")


def per_device(fields, weight_one, weight_two, edge_flips, cotangent):
    chans = fields.shape[1]
    tile = struct(chans, ROWS, LANES)
    flat = struct(chans, CELLS)
    pads = struct(3 * chans, PADDED)
    scratch = [pltpu.VMEM((3 * chans, PADDED), BF16)]
    field, cot, *rim = call(
        prepare_kernel,
        (flat, flat) + rim_shapes(chans),
        (edge_flips, fields.reshape(tile.shape), cotangent.reshape(tile.shape)),
    )
    halo = exchange(rim)
    sums = struct(*flat.shape, dtype=F32)
    pads_in, hidden, back_act = call(
        inner_kernel,
        (pads, sums, sums),
        (field, cot, weight_one, weight_two) + halo[:2],
        scratch,
        flags=False,
    )
    ends = pltpu.VMEM((3 * chans, 2 * LANES), BF16)
    shapes = (flat, flat, pads) + rim_shapes(chans)
    act, back, pads_in, *rim = pl.pallas_call(
        hidden_kernel,
        name="hidden",
        out_shape=shapes,
        in_specs=[SMEM, ANY] + [VMEM] * 6,
        out_specs=[VMEM, VMEM, ANY] + [VMEM] * (len(shapes) - 3),
        input_output_aliases={1: 2},
        scratch_shapes=[ends, ends, pltpu.SemaphoreType.DMA((2,))],
        compiler_params=pltpu.CompilerParams(vmem_limit_bytes=56 * 1024 * 1024),
    )(edge_flips, pads_in, hidden, back_act, weight_one, weight_two, *halo[2:])
    halo = exchange(rim)
    local = (struct(9 * chans, LANES, dtype=F32), struct(9 * chans, LANES))
    halves = [pltpu.VMEM((2, 9 * chans, LANES), F32)]
    one = call(grad_kernel, local, (back, pads_in), halves, flags=False)
    one = fold(one)
    pads_act, *two = call(grad_two_kernel, (pads,) + local, (edge_flips, act, cot) + halo, halves)
    two = fold(two)
    output = call(output_kernel, tile, (field, weight_two, pads_act), flags=False)
    quarter = reduce_grads(one, two)
    other = beside(quarter)
    grad_fields = call(
        grad_fields_kernel, tile, (edge_flips, cot, back, weight_one) + halo, scratch
    )
    pair = paired(quarter)
    across = paired(other)
    grads = finish(True, quarter, other)
    grad_one, grad_two = finish(False, pair, across, *grads)
    return (output.reshape(fields.shape), grad_fields.reshape(fields.shape), grad_one, grad_two)


def solution(mesh):
    in_specs = (P("dp", None, "lat", "lon"), P(), P(), P(), P("dp", None, "lat", "lon"))
    out_specs = (P("dp", None, "lat", "lon"), P("dp", None, "lat", "lon"), P(), P())


    return jax.shard_map(
        per_device, mesh=mesh, in_specs=in_specs, out_specs=out_specs, check_vma=False
    )
```

```python
import functools

import jax
import jax.numpy as jnp
from jax import lax
from jax.experimental import pallas as pl
from jax.experimental.pallas import tpu as pltpu
from jax.sharding import PartitionSpec as P


F32 = jnp.float32
BF16 = jnp.bfloat16
LANES = 128
ROWS = 8
CELLS = ROWS * LANES
PADDED = CELLS + 2 * LANES
NT = (((1,), (1,)), ((), ()))
TN = (((0,), (0,)), ((), ()))


def iota(shape, dim):
    return lax.broadcasted_iota(jnp.int32, shape, dim)


def one_hot(cond):
    return jnp.where(cond, 1.0, 0.0).astype(BF16)


def dot(a, b):
    return jnp.dot(a, b, preferred_element_type=F32)


def edge_flags(flips):
    a, o = (lax.axis_index("lat"), lax.axis_index("lon"))
    edges, lons = flips.shape

    def upper(col):
        return jnp.where(a > 0, flips[jnp.maximum(a - 1, 0), col], 0)

    def lower(col):
        return jnp.where(a < edges, flips[jnp.minimum(a, edges - 1), col], 0)

    west, east = (lax.rem(o + lons - 1, lons), lax.rem(o + 1, lons))
    return (upper(o), lower(o), upper(west), upper(east), lower(west), lower(east))


def rims(first, second, flags, outs):
    east, west, south, north = outs
    shape = (2 * ROWS, CELLS)
    row, cell = (iota(shape, 0), iota(shape, 1))
    pick = one_hot(cell == jnp.where(row < ROWS, row * LANES + LANES - 1, (row - ROWS) * LANES))
    one = lax.dot_general(pick, first, NT, preferred_element_type=F32)
    two = lax.dot_general(pick, second, NT, preferred_element_type=F32)
    chans = first.shape[0]
    upper, lower = (flags[0] == 1, flags[1] == 1)
    end = ROWS - 1

    def side(out, base, far):
        top = jnp.where(upper, two[far : far + 1], two[base : base + 1])
        low = jnp.where(lower, two[far + end : far + ROWS], two[base + end : base + ROWS])
        at = iota((ROWS, chans), 0)
        corners = jnp.where(at == 0, jnp.broadcast_to(top, at.shape), jnp.broadcast_to(low, at.shape))
        out[...] = jnp.concatenate(
            [one[base : base + ROWS], two[base : base + ROWS], corners, corners], 0
        ).astype(BF16)

    side(east, 0, ROWS)
    side(west, ROWS, 0)
    south[:chans] = first[:, CELLS - LANES :]
    south[chans : 2 * chans] = second[:, CELLS - LANES :]
    north[:chans] = first[:, :LANES]
    north[chans : 2 * chans] = second[:, :LANES]


def join_kernel(south, north, from_w, from_e, south_out, north_out, block, sems):
    rows = south_out.shape[0] - 32
    west, east = (from_w[...].astype(F32), from_e[...].astype(F32))
    at = iota((16, west.shape[1]), 0)
    copies = []
    for index, (out, near, corner) in enumerate(((south_out, 7, 17), (north_out, 0, 16))):
        spread = [
            jnp.broadcast_to(side[k : k + 1], at.shape)
            for side in (west, east)
            for k in (near, corner)
        ]
        cells = jnp.where(
            at == 0, spread[0], jnp.where(at == 1, spread[1], jnp.where(at == 2, spread[2], spread[3]))
        ).astype(BF16)
        block[index, :16] = cells[:, :LANES]
        block[index, 16:] = cells[:, LANES:]
        copies.append(
            pltpu.make_async_copy(block.at[index], out.at[pl.ds(rows, 32)], sems.at[index])
        )
        copies[-1].start()
    for copy in copies:
        copy.wait()


def corners_of(line, chans):
    rows = 2 * chans
    return jnp.concatenate([line[rows : rows + 16], line[rows + 16 : rows + 32]], 1)


def turned(line, flip):
    shape = (LANES, LANES)
    a, b = (iota(shape, 0), iota(shape, 1))
    turn = one_hot(b == a + flip * (LANES - 1 - 2 * a))
    return dot(line, turn)


def shifted(out, centre, top, bottom, west, east, swaps=(None, None), edges=False):
    swap_top, swap_bottom = swaps
    chans = west.shape[1]
    order = (0, 1, 2) if swap_top is None else (2, 1, 0)
    k, lane = (iota((16, PADDED), 0), iota((16, PADDED), 1))
    placed_west = lax.dot_general(
        west, one_hot(lane == k * LANES), TN, preferred_element_type=F32
    )
    placed_east = lax.dot_general(
        east, one_hot(lane == k * LANES + LANES - 1), TN, preferred_element_type=F32
    )
    lane_in = iota((chans, LANES), 1)
    for block in (0, ROWS + 1) if edges else range(ROWS + 2):
        span = slice(block * LANES, (block + 1) * LANES)
        to = slice(LANES, 2 * LANES) if edges and block else span
        if top is None and block in (0, ROWS + 1):
            out[:, span] = jnp.zeros((3 * chans, LANES), BF16)
            continue
        if block == 0:
            line = top
        elif block == ROWS + 1:
            line = bottom
        else:
            line = centre[:, (block - 1) * LANES : block * LANES].astype(F32)
        left = jnp.where(lane_in == 0, placed_west[:, span], pltpu.roll(line, 1, 1))
        right = jnp.where(lane_in == LANES - 1, placed_east[:, span], pltpu.roll(line, LANES - 1, 1))
        swap = swap_top if block == 0 else swap_bottom if block == ROWS + 1 else None
        if swap is not None:
            left, right = (jnp.where(swap, right, left), jnp.where(swap, left, right))
        for slot, cells in zip(order, (left, line, right)):
            out[slot * chans : (slot + 1) * chans, to] = cells.astype(BF16)


def lines(top, mid, bottom):
    return jnp.concatenate([top, mid, bottom, jnp.zeros((6, mid.shape[1]), F32)], 0).astype(BF16)


def pad_forward(out, centre, flags, halo, part=None):
    from_w, from_e, from_n, from_s = halo
    chans = out.shape[0] // 3
    sides = [jnp.zeros((ROWS, chans), F32)] * 2
    if part != "edges":
        sides = [ref[...].astype(F32)[:ROWS] for ref in (from_w, from_e)]
    if part == "inner":
        none = jnp.zeros((1, chans), F32)
        west, east = (lines(none, side, none) for side in sides)
        shifted(out, centre, None, None, west, east)
        return
    upper, lower = (flags[0] == 1, flags[1] == 1)
    above, below = (corners_of(ref, chans).astype(F32) for ref in (from_n, from_s))
    nw, ne, sw, se = (above[:1], above[2:3], below[:1], below[2:3])
    west = lines(jnp.where(upper, ne, nw), sides[0], jnp.where(lower, se, sw))
    east = lines(jnp.where(upper, nw, ne), sides[1], jnp.where(lower, sw, se))
    top = turned(from_n[:chans], flags[0])
    bottom = turned(from_s[:chans], flags[1])
    shifted(out, centre, top, bottom, west, east, edges=part == "edges")


def pad_backward(out, centre, flags, halo, part=None):
    from_w, from_e, from_n, from_s = halo
    chans = out.shape[0] // 3
    none = jnp.zeros((1, chans), F32)
    sides = [jnp.zeros((ROWS, chans), F32)] * 2
    if part != "edges":
        sides = [ref[...].astype(F32)[ROWS : 2 * ROWS] for ref in (from_w, from_e)]
    west, east = (lines(none, side, none) for side in sides)
    if part == "inner":
        shifted(out, centre, None, None, west, east, (False, False))
        return
    upper, lower = (flags[0] == 1, flags[1] == 1)
    top = turned(from_n[chans : 2 * chans], flags[0])
    bottom = turned(from_s[chans : 2 * chans], flags[1])
    shifted(out, centre, top, bottom, west, east, (upper, lower), part == "edges")


def conv(weight, pads):
    total = None
    for r in range(3):
        taps = jnp.concatenate([weight[3 * r + s] for s in range(3)], 1)
        term = dot(taps, pads[:, r * LANES : r * LANES + CELLS])
        total = term if total is None else total + term
    return total


def adjoint_rows(weight, r, cells):
    taps = jnp.concatenate([weight[3 * r + s] for s in range(3)], 0)
    return lax.dot_general(taps, cells, TN, preferred_element_type=F32)


def adjoint_corners(weight, flags, halo, chans):
    above, below = (corners_of(ref, chans) for ref in halo[2:])
    k, lane = (iota((16, LANES), 0), iota((16, LANES), 1))

    def corner(block, which, at, tap):
        spread = lax.dot_general(
            block, one_hot((k == which) & (lane == at)), TN, preferred_element_type=F32
        ).astype(BF16)
        return lax.dot_general(weight[tap], spread, TN, preferred_element_type=F32)

    east = LANES - 1
    top = corner(above, 1, 0, 8 - 2 * flags[2]) + corner(above, 3, east, 6 + 2 * flags[3])
    bottom = corner(below, 1, 0, 2 - 2 * flags[4]) + corner(below, 3, east, 2 * flags[5])
    return (top, bottom)


def with_ends(total, top, bottom):
    return jnp.concatenate(
        [total[:, :LANES] + top, total[:, LANES : CELLS - LANES], total[:, CELLS - LANES :] + bottom],
        1,
    )


def adjoint_inner(weight, pads):
    total = None
    for r in range(3):
        start = (2 - r) * LANES
        term = adjoint_rows(weight, r, pads[:, start : start + CELLS])
        total = term if total is None else total + term
    return total


def conv_adjoint(weight, pads, flags, halo):
    total = adjoint_inner(weight, pads)
    return with_ends(total, *adjoint_corners(weight, flags, halo, total.shape[0]))


def prepare_kernel(flips, field, cotangent, *outs):
    flat_field, flat_cot = outs[:2]
    for row in range(ROWS):
        span = slice(row * LANES, (row + 1) * LANES)
        flat_field[:, span] = field[:, row, :]
        flat_cot[:, span] = cotangent[:, row, :]
    rims(flat_field[...], flat_cot[...], edge_flags(flips), outs[2:])


def inner_kernel(field, cotangent, one, two, from_w, from_e, pads, hidden, back_act, back_pads):
    halo = (from_w, from_e, None, None)
    pad_forward(pads, field[...], None, halo, "inner")
    hidden[...] = conv(one, pads)
    pad_backward(back_pads, cotangent[...], None, halo, "inner")
    back_act[...] = adjoint_inner(two, back_pads)


def hidden_kernel(flips, pads_in, hidden_in, back_in, one, two, from_n, from_s, *refs):
    act_out, back_out, pads_out = refs[:3]
    ends, back_ends, sems = refs[-3:]
    flags = edge_flags(flips)
    halo = (None, None, from_n, from_s)
    chans = hidden_in.shape[0]
    pad_forward(ends, None, flags, halo, "edges")
    copies = [
        pltpu.make_async_copy(
            ends.at[:, pl.ds(k * LANES, LANES)],
            pads_out.at[:, pl.ds(k * (PADDED - LANES), LANES)],
            sems.at[k],
        )
        for k in range(2)
    ]
    for copy in copies:
        copy.start()
    pad_backward(back_ends, None, flags, halo, "edges")
    first, last = (jnp.concatenate([one[k + s] for s in range(3)], 1) for k in (0, 6))
    hidden = with_ends(
        hidden_in[...], dot(first, ends[:, :LANES]), dot(last, ends[:, LANES:])
    )
    top, bottom = adjoint_corners(two, flags, halo, chans)
    back_act = with_ends(
        back_in[...],
        top + adjoint_rows(two, 2, back_ends[:, :LANES]),
        bottom + adjoint_rows(two, 0, back_ends[:, LANES:]),
    )
    sigma = 1.0 / (1.0 + jnp.exp(-hidden))
    act_out[...] = (hidden * sigma).astype(BF16)
    back_out[...] = (back_act * sigma * (1.0 + hidden * (1.0 - sigma))).astype(BF16)
    rims(act_out[...], back_out[...], flags, refs[3:-3])
    for copy in copies:
        copy.wait()


def grad_kernel(grad_tile, pads, keep, away, both):
    core = lax.rem(lax.axis_index("dp"), 2)
    chans = grad_tile.shape[0]
    for r in range(3):
        terms = lax.dot_general(
            grad_tile[...], pads[:, r * LANES : r * LANES + CELLS], NT, preferred_element_type=F32
        )
        for piece in range(6):
            half, group = divmod(6 * r + piece, 9)
            place = core if half == 0 else 1 - core
            rows = slice(group * chans, (group + 1) * chans)
            both[place, rows] = terms[:, piece * LANES : (piece + 1) * LANES]
    keep[...] = both[0]
    away[...] = both[1].astype(BF16)


def grad_two_kernel(flips, act, cotangent, *refs):
    halo, pads, outs = (refs[:4], refs[4], refs[5:])
    pad_forward(pads, act[...], edge_flags(flips), halo)
    grad_kernel(cotangent, pads, *outs)


def output_kernel(field, weight, pads, output):
    total = (field[...].astype(F32) + conv(weight, pads)).astype(BF16)
    for row in range(ROWS):
        output[:, row, :] = total[:, row * LANES : (row + 1) * LANES]


def grad_fields_kernel(flips, cotangent, back, weight, *refs):
    halo, (grad_fields, back_pads) = (refs[:4], refs[4:])
    flags = edge_flags(flips)
    pad_backward(back_pads, back[...], flags, halo)
    total = (cotangent[...].astype(F32) + conv_adjoint(weight, back_pads, flags, halo)).astype(BF16)
    for row in range(ROWS):
        grad_fields[:, row, :] = total[:, row * LANES : (row + 1) * LANES]


def quarter_kernel(own_core, own_side, quarter, *refs):
    outs, (flat, stage, got, sems) = (refs[-6:-4], refs[-4:])
    place = lax.axis_index("dp")
    side, core = (lax.shift_right_logical(place, 1), lax.rem(place, 2))
    half = core if own_core else 1 - core
    part = side if own_side else 1 - side
    chans = stage.shape[2]
    tiles, depth = quarter.shape[:2]
    depth = depth // 2
    size = tiles * depth
    loads = [
        pltpu.make_async_copy(
            quarter.at[tile, pl.ds(which * depth, depth), :],
            flat.at[which, pl.ds(tile * depth, depth), :],
            got.at[which, tile],
        )
        for which in range(2)
        for tile in range(tiles)
    ]
    for load in loads:
        load.start()
    for load in loads:
        load.wait()

    def place_quarter(half_at, part_at):
        copies = []
        base = part_at * size
        for which, out in enumerate(outs):
            slot = 0
            for group in range(9):
                low, high = (max(group * chans, base), min((group + 1) * chans, base + size))
                if high <= low:
                    continue
                tap, lanes = divmod(group + 9 * half_at, 2)
                count = high - low
                stage[which, slot, :count] = flat[which, low - base : high - base].astype(F32)
                copies.append(
                    pltpu.make_async_copy(
                        stage.at[which, slot, pl.ds(0, count), :],
                        out.at[tap, pl.ds(low - group * chans, count), pl.ds(lanes * LANES, LANES)],
                        sems.at[which, slot],
                    )
                )
                copies[-1].start()
                slot += 1
        for copy in copies:
            copy.wait()

    for half_at in range(2):
        for part_at in range(2):
            pl.when((half == half_at) & (part == part_at))(
                functools.partial(place_quarter, half_at, part_at)
            )


def finish(own_core, own_side, quarter, *partial):
    chans = 2 * LANES
    grad = struct(9, chans, chans, dtype=F32)
    return pl.pallas_call(
        functools.partial(quarter_kernel, own_core, own_side),
        out_shape=(grad, grad),
        in_specs=[ANY] * (1 + len(partial)),
        out_specs=(ANY, ANY),
        input_output_aliases={1 + k: k for k in range(len(partial))},
        scratch_shapes=[
            pltpu.VMEM((2, 9 * chans // 2, LANES), BF16),
            pltpu.VMEM((2, 5, chans, LANES), F32),
            pltpu.SemaphoreType.DMA((2, quarter.shape[0])),
            pltpu.SemaphoreType.DMA((2, 5)),
        ],
    )(quarter, *partial)


SMEM = pl.BlockSpec(memory_space=pltpu.SMEM)
VMEM = pl.BlockSpec(memory_space=pltpu.VMEM)
ANY = pl.BlockSpec(memory_space=pl.ANY)


def call(kernel, out_shape, args, scratch=(), flags=True):
    return pl.pallas_call(
        kernel,
        out_shape=out_shape,
        in_specs=([SMEM] if flags else []) + [VMEM] * (len(args) - (1 if flags else 0)),
        out_specs=jax.tree.map(lambda _: VMEM, out_shape),
        scratch_shapes=list(scratch),
        compiler_params=pltpu.CompilerParams(vmem_limit_bytes=56 * 1024 * 1024),
    )(*args)


def struct(*shape, dtype=BF16):
    return jax.ShapeDtypeStruct(shape, dtype)


def rim_shapes(chans):
    side = struct(4 * ROWS, chans)
    line = struct(2 * chans + 32, LANES)
    return (side, side, line, line)


def exchange(rim):
    east, west, south, north = rim
    lons, lats = (lax.axis_size("lon"), lax.axis_size("lat"))

    def along(value, step):
        return lax.ppermute(value, "lon", [(i, (i + step) % lons) for i in range(lons)])

    def across(value, step):
        return lax.ppermute(
            value, "lat", [(i, i + step) for i in range(lats) if 0 <= i + step < lats]
        )

    from_w, from_e = (along(east, 1), along(west, -1))
    line = struct(*south.shape)
    south, north = pl.pallas_call(
        join_kernel,
        name="join",
        out_shape=(line, line),
        in_specs=[ANY, ANY, VMEM, VMEM],
        out_specs=(ANY, ANY),
        input_output_aliases={0: 0, 1: 1},
        scratch_shapes=[pltpu.VMEM((2, 32, LANES), BF16), pltpu.SemaphoreType.DMA((2,))],
    )(south, north, from_w, from_e)
    from_n = across(south, 1)
    from_s = across(north, -1)
    return (from_w, from_e, from_n, from_s)


def beside(value):
    return lax.ppermute(value, "dp", [(i, (i + 2) % 4) for i in range(4)])


def paired(value):
    return lax.ppermute(value, "dp", [(0, 1), (1, 0), (2, 3), (3, 2)])


def over(value, axis):
    return lax.all_to_all(value, axis, 0, 0)


def total(parts):
    return jnp.sum(parts.astype(F32), 0)


def fold(grad):
    keep, away = grad
    got = paired(away)
    side = lax.shift_right_logical(lax.axis_index("dp"), 1)
    half = keep.shape[0] // 2

    def rows(which):
        pick = lambda value: lax.dynamic_slice_in_dim(value, which * half, half, 0).astype(F32)
        return pick(keep) + pick(got)

    return (rows(side), beside(rows(1 - side).astype(BF16)))


def gathered(value, axis):
    return over(jnp.broadcast_to(value[None], (lax.axis_size(axis),) + value.shape), axis)


def reduce_grads(one, two):
    lats, lons = (lax.axis_size("lat"), lax.axis_size("lon"))
    parts = [
        (kept + got.astype(F32)).astype(BF16).reshape(lats, -1, LANES) for kept, got in (one, two)
    ]
    share = total(over(jnp.concatenate(parts, 1), "lat"))
    share = total(over(share.reshape(lons, share.shape[0] // lons, LANES), "lon")).astype(BF16)
    share = gathered(share, "lon")
    return gathered(share.reshape(-1, LANES), "lat")


def per_device(fields, weight_one, weight_two, edge_flips, cotangent):
    chans = fields.shape[1]
    tile = struct(chans, ROWS, LANES)
    flat = struct(chans, CELLS)
    pads = struct(3 * chans, PADDED)
    scratch = [pltpu.VMEM((3 * chans, PADDED), BF16)]
    field, cot, *rim = call(
        prepare_kernel,
        (flat, flat) + rim_shapes(chans),
        (edge_flips, fields.reshape(tile.shape), cotangent.reshape(tile.shape)),
    )
    halo = exchange(rim)
    sums = struct(*flat.shape, dtype=F32)
    pads_in, hidden, back_act = call(
        inner_kernel,
        (pads, sums, sums),
        (field, cot, weight_one, weight_two) + halo[:2],
        scratch,
        flags=False,
    )
    ends = pltpu.VMEM((3 * chans, 2 * LANES), BF16)
    shapes = (flat, flat, pads) + rim_shapes(chans)
    act, back, pads_in, *rim = pl.pallas_call(
        hidden_kernel,
        name="hidden",
        out_shape=shapes,
        in_specs=[SMEM, ANY] + [VMEM] * 6,
        out_specs=[VMEM, VMEM, ANY] + [VMEM] * (len(shapes) - 3),
        input_output_aliases={1: 2},
        scratch_shapes=[ends, ends, pltpu.SemaphoreType.DMA((2,))],
        compiler_params=pltpu.CompilerParams(vmem_limit_bytes=56 * 1024 * 1024),
    )(edge_flips, pads_in, hidden, back_act, weight_one, weight_two, *halo[2:])
    halo = exchange(rim)
    local = (struct(9 * chans, LANES, dtype=F32), struct(9 * chans, LANES))
    halves = [pltpu.VMEM((2, 9 * chans, LANES), F32)]
    one = call(grad_kernel, local, (back, pads_in), halves, flags=False)
    one = fold(one)
    pads_act, *two = call(grad_two_kernel, (pads,) + local, (edge_flips, act, cot) + halo, halves)
    two = fold(two)
    output = call(output_kernel, tile, (field, weight_two, pads_act), flags=False)
    quarter = reduce_grads(one, two)
    other = beside(quarter)
    grad_fields = call(
        grad_fields_kernel, tile, (edge_flips, cot, back, weight_one) + halo, scratch
    )
    pair = paired(quarter)
    across = paired(other)
    grads = finish(True, True, quarter)
    grads = finish(False, True, pair, *grads)
    grads = finish(True, False, other, *grads)
    grad_one, grad_two = finish(False, False, across, *grads)
    return (output.reshape(fields.shape), grad_fields.reshape(fields.shape), grad_one, grad_two)


def solution(mesh):
    in_specs = (P("dp", None, "lat", "lon"), P(), P(), P(), P("dp", None, "lat", "lon"))
    out_specs = (P("dp", None, "lat", "lon"), P("dp", None, "lat", "lon"), P(), P())


    return jax.shard_map(
        per_device, mesh=mesh, in_specs=in_specs, out_specs=out_specs, check_vma=False
    )
```

```python
import functools

import jax
import jax.numpy as jnp
from jax import lax
from jax.experimental import pallas as pl
from jax.experimental.pallas import tpu as pltpu
from jax.sharding import PartitionSpec as P


F32 = jnp.float32
BF16 = jnp.bfloat16
LANES = 128
ROWS = 8
CELLS = ROWS * LANES
PADDED = CELLS + 2 * LANES
NT = (((1,), (1,)), ((), ()))
TN = (((0,), (0,)), ((), ()))


def iota(shape, dim):
    return lax.broadcasted_iota(jnp.int32, shape, dim)


def one_hot(cond):
    return jnp.where(cond, 1.0, 0.0).astype(BF16)


def dot(a, b):
    return jnp.dot(a, b, preferred_element_type=F32)


def edge_flags(flips):
    a, o = (lax.axis_index("lat"), lax.axis_index("lon"))
    edges, lons = flips.shape

    def upper(col):
        return jnp.where(a > 0, flips[jnp.maximum(a - 1, 0), col], 0)

    def lower(col):
        return jnp.where(a < edges, flips[jnp.minimum(a, edges - 1), col], 0)

    west, east = (lax.rem(o + lons - 1, lons), lax.rem(o + 1, lons))
    return (upper(o), lower(o), upper(west), upper(east), lower(west), lower(east))


def rims(first, second, flags, outs):
    east, west, south, north = outs
    shape = (2 * ROWS, CELLS)
    row, cell = (iota(shape, 0), iota(shape, 1))
    pick = one_hot(cell == jnp.where(row < ROWS, row * LANES + LANES - 1, (row - ROWS) * LANES))
    one = lax.dot_general(pick, first, NT, preferred_element_type=F32)
    two = lax.dot_general(pick, second, NT, preferred_element_type=F32)
    chans = first.shape[0]
    upper, lower = (flags[0] == 1, flags[1] == 1)
    end = ROWS - 1

    def side(out, base, far):
        top = jnp.where(upper, two[far : far + 1], two[base : base + 1])
        low = jnp.where(lower, two[far + end : far + ROWS], two[base + end : base + ROWS])
        at = iota((ROWS, chans), 0)
        corners = jnp.where(at == 0, jnp.broadcast_to(top, at.shape), jnp.broadcast_to(low, at.shape))
        out[...] = jnp.concatenate(
            [one[base : base + ROWS], two[base : base + ROWS], corners, corners], 0
        ).astype(BF16)

    side(east, 0, ROWS)
    side(west, ROWS, 0)
    south[:chans] = first[:, CELLS - LANES :]
    south[chans : 2 * chans] = second[:, CELLS - LANES :]
    north[:chans] = first[:, :LANES]
    north[chans : 2 * chans] = second[:, :LANES]


def join_kernel(south, north, from_w, from_e, south_out, north_out, block, sems):
    rows = south_out.shape[0] - 32
    west, east = (from_w[...].astype(F32), from_e[...].astype(F32))
    at = iota((16, west.shape[1]), 0)
    copies = []
    for index, (out, near, corner) in enumerate(((south_out, 7, 17), (north_out, 0, 16))):
        spread = [
            jnp.broadcast_to(side[k : k + 1], at.shape)
            for side in (west, east)
            for k in (near, corner)
        ]
        cells = jnp.where(
            at == 0, spread[0], jnp.where(at == 1, spread[1], jnp.where(at == 2, spread[2], spread[3]))
        ).astype(BF16)
        block[index, :16] = cells[:, :LANES]
        block[index, 16:] = cells[:, LANES:]
        copies.append(
            pltpu.make_async_copy(block.at[index], out.at[pl.ds(rows, 32)], sems.at[index])
        )
        copies[-1].start()
    for copy in copies:
        copy.wait()


def corners_of(line, chans):
    rows = 2 * chans
    return jnp.concatenate([line[rows : rows + 16], line[rows + 16 : rows + 32]], 1)


def turned(line, flip):
    shape = (LANES, LANES)
    a, b = (iota(shape, 0), iota(shape, 1))
    turn = one_hot(b == a + flip * (LANES - 1 - 2 * a))
    return dot(line, turn)


def shifted(out, centre, top, bottom, west, east, swaps=(None, None), edges=False):
    swap_top, swap_bottom = swaps
    chans = west.shape[1]
    order = (0, 1, 2) if swap_top is None else (2, 1, 0)
    k, lane = (iota((16, PADDED), 0), iota((16, PADDED), 1))
    placed_west = lax.dot_general(
        west, one_hot(lane == k * LANES), TN, preferred_element_type=F32
    )
    placed_east = lax.dot_general(
        east, one_hot(lane == k * LANES + LANES - 1), TN, preferred_element_type=F32
    )
    lane_in = iota((chans, LANES), 1)
    for block in (0, ROWS + 1) if edges else range(ROWS + 2):
        span = slice(block * LANES, (block + 1) * LANES)
        to = slice(LANES, 2 * LANES) if edges and block else span
        if top is None and block in (0, ROWS + 1):
            out[:, span] = jnp.zeros((3 * chans, LANES), BF16)
            continue
        if block == 0:
            line = top
        elif block == ROWS + 1:
            line = bottom
        else:
            line = centre[:, (block - 1) * LANES : block * LANES].astype(F32)
        left = jnp.where(lane_in == 0, placed_west[:, span], pltpu.roll(line, 1, 1))
        right = jnp.where(lane_in == LANES - 1, placed_east[:, span], pltpu.roll(line, LANES - 1, 1))
        swap = swap_top if block == 0 else swap_bottom if block == ROWS + 1 else None
        if swap is not None:
            left, right = (jnp.where(swap, right, left), jnp.where(swap, left, right))
        for slot, cells in zip(order, (left, line, right)):
            out[slot * chans : (slot + 1) * chans, to] = cells.astype(BF16)


def lines(top, mid, bottom):
    return jnp.concatenate([top, mid, bottom, jnp.zeros((6, mid.shape[1]), F32)], 0).astype(BF16)


def pad_forward(out, centre, flags, halo, part=None):
    from_w, from_e, from_n, from_s = halo
    chans = out.shape[0] // 3
    sides = [jnp.zeros((ROWS, chans), F32)] * 2
    if part != "edges":
        sides = [ref[...].astype(F32)[:ROWS] for ref in (from_w, from_e)]
    if part == "inner":
        none = jnp.zeros((1, chans), F32)
        west, east = (lines(none, side, none) for side in sides)
        shifted(out, centre, None, None, west, east)
        return
    upper, lower = (flags[0] == 1, flags[1] == 1)
    above, below = (corners_of(ref, chans).astype(F32) for ref in (from_n, from_s))
    nw, ne, sw, se = (above[:1], above[2:3], below[:1], below[2:3])
    west = lines(jnp.where(upper, ne, nw), sides[0], jnp.where(lower, se, sw))
    east = lines(jnp.where(upper, nw, ne), sides[1], jnp.where(lower, sw, se))
    top = turned(from_n[:chans], flags[0])
    bottom = turned(from_s[:chans], flags[1])
    shifted(out, centre, top, bottom, west, east, edges=part == "edges")


def pad_backward(out, centre, flags, halo, part=None):
    from_w, from_e, from_n, from_s = halo
    chans = out.shape[0] // 3
    none = jnp.zeros((1, chans), F32)
    sides = [jnp.zeros((ROWS, chans), F32)] * 2
    if part != "edges":
        sides = [ref[...].astype(F32)[ROWS : 2 * ROWS] for ref in (from_w, from_e)]
    west, east = (lines(none, side, none) for side in sides)
    if part == "inner":
        shifted(out, centre, None, None, west, east, (False, False))
        return
    upper, lower = (flags[0] == 1, flags[1] == 1)
    top = turned(from_n[chans : 2 * chans], flags[0])
    bottom = turned(from_s[chans : 2 * chans], flags[1])
    shifted(out, centre, top, bottom, west, east, (upper, lower), part == "edges")


def conv(weight, pads):
    total = None
    for r in range(3):
        taps = jnp.concatenate([weight[3 * r + s] for s in range(3)], 1)
        term = dot(taps, pads[:, r * LANES : r * LANES + CELLS])
        total = term if total is None else total + term
    return total


def adjoint_rows(weight, r, cells):
    taps = jnp.concatenate([weight[3 * r + s] for s in range(3)], 0)
    return lax.dot_general(taps, cells, TN, preferred_element_type=F32)


def adjoint_corners(weight, flags, halo, chans):
    above, below = (corners_of(ref, chans) for ref in halo[2:])
    k, lane = (iota((16, LANES), 0), iota((16, LANES), 1))

    def corner(block, which, at, tap):
        spread = jnp.where((k == which) & (lane == at), 1.0, 0.0)
        return lax.dot_general(
            dot(block, weight[tap]),
            spread,
            TN,
            precision=lax.Precision.HIGHEST,
            preferred_element_type=F32,
        )

    east = LANES - 1
    top = corner(above, 1, 0, 8 - 2 * flags[2]) + corner(above, 3, east, 6 + 2 * flags[3])
    bottom = corner(below, 1, 0, 2 - 2 * flags[4]) + corner(below, 3, east, 2 * flags[5])
    return (top, bottom)


def with_ends(total, top, bottom):
    return jnp.concatenate(
        [total[:, :LANES] + top, total[:, LANES : CELLS - LANES], total[:, CELLS - LANES :] + bottom],
        1,
    )


def adjoint_inner(weight, pads):
    total = None
    for r in range(3):
        start = (2 - r) * LANES
        term = adjoint_rows(weight, r, pads[:, start : start + CELLS])
        total = term if total is None else total + term
    return total


def conv_adjoint(weight, pads, flags, halo):
    total = adjoint_inner(weight, pads)
    return with_ends(total, *adjoint_corners(weight, flags, halo, total.shape[0]))


def prepare_kernel(flips, field, cotangent, *outs):
    flat_field, flat_cot = outs[:2]
    for row in range(ROWS):
        span = slice(row * LANES, (row + 1) * LANES)
        flat_field[:, span] = field[:, row, :]
        flat_cot[:, span] = cotangent[:, row, :]
    rims(flat_field[...], flat_cot[...], edge_flags(flips), outs[2:])


def inner_kernel(field, cotangent, one, two, from_w, from_e, pads, hidden, back_act, back_pads):
    halo = (from_w, from_e, None, None)
    pad_forward(pads, field[...], None, halo, "inner")
    hidden[...] = conv(one, pads)
    pad_backward(back_pads, cotangent[...], None, halo, "inner")
    back_act[...] = adjoint_inner(two, back_pads)


def hidden_kernel(flips, pads_in, hidden_in, back_in, one, two, from_n, from_s, *refs):
    act_out, back_out, pads_out = refs[:3]
    ends, back_ends, sems = refs[-3:]
    flags = edge_flags(flips)
    halo = (None, None, from_n, from_s)
    chans = hidden_in.shape[0]
    pad_forward(ends, None, flags, halo, "edges")
    copies = [
        pltpu.make_async_copy(
            ends.at[:, pl.ds(k * LANES, LANES)],
            pads_out.at[:, pl.ds(k * (PADDED - LANES), LANES)],
            sems.at[k],
        )
        for k in range(2)
    ]
    for copy in copies:
        copy.start()
    pad_backward(back_ends, None, flags, halo, "edges")
    first, last = (jnp.concatenate([one[k + s] for s in range(3)], 1) for k in (0, 6))
    hidden = with_ends(
        hidden_in[...], dot(first, ends[:, :LANES]), dot(last, ends[:, LANES:])
    )
    top, bottom = adjoint_corners(two, flags, halo, chans)
    back_act = with_ends(
        back_in[...],
        top + adjoint_rows(two, 2, back_ends[:, :LANES]),
        bottom + adjoint_rows(two, 0, back_ends[:, LANES:]),
    )
    sigma = 1.0 / (1.0 + jnp.exp(-hidden))
    act_out[...] = (hidden * sigma).astype(BF16)
    back_out[...] = (back_act * sigma * (1.0 + hidden * (1.0 - sigma))).astype(BF16)
    rims(act_out[...], back_out[...], flags, refs[3:-3])
    for copy in copies:
        copy.wait()


def grad_kernel(grad_tile, pads, keep, away, both):
    core = lax.rem(lax.axis_index("dp"), 2)
    chans = grad_tile.shape[0]
    for r in range(3):
        terms = lax.dot_general(
            grad_tile[...], pads[:, r * LANES : r * LANES + CELLS], NT, preferred_element_type=F32
        )
        for piece in range(6):
            half, group = divmod(6 * r + piece, 9)
            place = core if half == 0 else 1 - core
            rows = slice(group * chans, (group + 1) * chans)
            both[place, rows] = terms[:, piece * LANES : (piece + 1) * LANES]
    keep[...] = both[0]
    away[...] = both[1].astype(BF16)


def grad_two_kernel(flips, act, cotangent, *refs):
    halo, pads, outs = (refs[:4], refs[4], refs[5:])
    pad_forward(pads, act[...], edge_flags(flips), halo)
    grad_kernel(cotangent, pads, *outs)


def output_kernel(field, weight, pads, output):
    total = (field[...].astype(F32) + conv(weight, pads)).astype(BF16)
    for row in range(ROWS):
        output[:, row, :] = total[:, row * LANES : (row + 1) * LANES]


def grad_fields_kernel(flips, cotangent, back, weight, *refs):
    halo, (grad_fields, back_pads) = (refs[:4], refs[4:])
    flags = edge_flags(flips)
    pad_backward(back_pads, back[...], flags, halo)
    total = (cotangent[...].astype(F32) + conv_adjoint(weight, back_pads, flags, halo)).astype(BF16)
    for row in range(ROWS):
        grad_fields[:, row, :] = total[:, row * LANES : (row + 1) * LANES]


def finish_kernel(own, near, far, *refs):
    outs, (flat, stage, sems, got) = (refs[-6:-4], refs[-4:])
    place = lax.axis_index("dp")
    side, core = (lax.shift_right_logical(place, 1), lax.rem(place, 2))
    half = core if own else 1 - core
    chans = stage.shape[2]
    tiles, depth = near.shape[:2]
    depth = depth // 2
    size = tiles * depth
    loads = []
    for which in range(2):
        for tile in range(tiles):
            for index, (ref, to) in enumerate(((near, side), (far, 1 - side))):
                start = pl.multiple_of(to * size + tile * depth, 16)
                loads.append(
                    pltpu.make_async_copy(
                        ref.at[tile, pl.ds(which * depth, depth), :],
                        flat.at[which, pl.ds(start, depth), :],
                        got.at[which, tile, index],
                    )
                )
                loads[-1].start()
    for load in loads:
        load.wait()

    def place_half(odd):
        copies = []
        for which, out in enumerate(outs):
            for slot in range(5):
                lanes = slice(0, 2 * LANES)
                for part in range(2):
                    group = 2 * slot + part - odd
                    if 0 <= group < 9:
                        span = slice(part * LANES, (part + 1) * LANES)
                        rows = slice(group * chans, (group + 1) * chans)
                        stage[which, slot, :, span] = flat[which, rows].astype(F32)
                    else:
                        lanes = slice((1 - part) * LANES, (2 - part) * LANES)
                copies.append(
                    pltpu.make_async_copy(
                        stage.at[which, slot, :, lanes],
                        out.at[slot + 4 * odd, :, lanes],
                        sems.at[which, slot],
                    )
                )
                copies[-1].start()
        for copy in copies:
            copy.wait()

    @pl.when(half == 0)
    def _():
        place_half(0)

    @pl.when(half == 1)
    def _():
        place_half(1)


def finish(own, near, far, *partial):
    chans = partial[0].shape[1] if partial else 2 * LANES
    grad = struct(9, chans, chans, dtype=F32)
    return pl.pallas_call(
        functools.partial(finish_kernel, own),
        out_shape=(grad, grad),
        in_specs=[ANY, ANY] + [ANY] * len(partial),
        out_specs=(ANY, ANY),
        input_output_aliases={2 + k: k for k in range(len(partial))},
        scratch_shapes=[
            pltpu.VMEM((2, 9 * chans, LANES), BF16),
            pltpu.VMEM((2, 5, chans, chans), F32),
            pltpu.SemaphoreType.DMA((2, 5)),
            pltpu.SemaphoreType.DMA((2, near.shape[0], 2)),
        ],
        compiler_params=pltpu.CompilerParams(vmem_limit_bytes=56 * 1024 * 1024),
    )(near, far, *partial)


SMEM = pl.BlockSpec(memory_space=pltpu.SMEM)
VMEM = pl.BlockSpec(memory_space=pltpu.VMEM)
ANY = pl.BlockSpec(memory_space=pl.ANY)


def call(kernel, out_shape, args, scratch=(), flags=True):
    return pl.pallas_call(
        kernel,
        out_shape=out_shape,
        in_specs=([SMEM] if flags else []) + [VMEM] * (len(args) - (1 if flags else 0)),
        out_specs=jax.tree.map(lambda _: VMEM, out_shape),
        scratch_shapes=list(scratch),
        compiler_params=pltpu.CompilerParams(vmem_limit_bytes=56 * 1024 * 1024),
    )(*args)


def struct(*shape, dtype=BF16):
    return jax.ShapeDtypeStruct(shape, dtype)


def rim_shapes(chans):
    side = struct(4 * ROWS, chans)
    line = struct(2 * chans + 32, LANES)
    return (side, side, line, line)


def exchange(rim):
    east, west, south, north = rim
    lons, lats = (lax.axis_size("lon"), lax.axis_size("lat"))

    def along(value, step):
        return lax.ppermute(value, "lon", [(i, (i + step) % lons) for i in range(lons)])

    def across(value, step):
        return lax.ppermute(
            value, "lat", [(i, i + step) for i in range(lats) if 0 <= i + step < lats]
        )

    from_w, from_e = (along(east, 1), along(west, -1))
    line = struct(*south.shape)
    south, north = pl.pallas_call(
        join_kernel,
        name="join",
        out_shape=(line, line),
        in_specs=[ANY, ANY, VMEM, VMEM],
        out_specs=(ANY, ANY),
        input_output_aliases={0: 0, 1: 1},
        scratch_shapes=[pltpu.VMEM((2, 32, LANES), BF16), pltpu.SemaphoreType.DMA((2,))],
    )(south, north, from_w, from_e)
    from_n = across(south, 1)
    from_s = across(north, -1)
    return (from_w, from_e, from_n, from_s)


def beside(value):
    return lax.ppermute(value, "dp", [(i, (i + 2) % 4) for i in range(4)])


def paired(value):
    return lax.ppermute(value, "dp", [(0, 1), (1, 0), (2, 3), (3, 2)])


def over(value, axis):
    return lax.all_to_all(value, axis, 0, 0)


def total(parts):
    return jnp.sum(parts.astype(F32), 0)


def fold(grad):
    keep, away = grad
    got = paired(away)
    side = lax.shift_right_logical(lax.axis_index("dp"), 1)
    half = keep.shape[0] // 2

    def rows(which):
        pick = lambda value: lax.dynamic_slice_in_dim(value, which * half, half, 0).astype(F32)
        return pick(keep) + pick(got)

    return (rows(side), beside(rows(1 - side).astype(BF16)))


def gathered(value, axis):
    return over(jnp.broadcast_to(value[None], (lax.axis_size(axis),) + value.shape), axis)


def reduce_grads(one, two):
    lats, lons = (lax.axis_size("lat"), lax.axis_size("lon"))
    parts = [
        (kept + got.astype(F32)).astype(BF16).reshape(lats, -1, LANES) for kept, got in (one, two)
    ]
    share = total(over(jnp.concatenate(parts, 1), "lat"))
    share = total(over(share.reshape(lons, share.shape[0] // lons, LANES), "lon")).astype(BF16)
    share = gathered(share, "lon")
    return gathered(share.reshape(-1, LANES), "lat")


def per_device(fields, weight_one, weight_two, edge_flips, cotangent):
    chans = fields.shape[1]
    tile = struct(chans, ROWS, LANES)
    flat = struct(chans, CELLS)
    pads = struct(3 * chans, PADDED)
    scratch = [pltpu.VMEM((3 * chans, PADDED), BF16)]
    field, cot, *rim = call(
        prepare_kernel,
        (flat, flat) + rim_shapes(chans),
        (edge_flips, fields.reshape(tile.shape), cotangent.reshape(tile.shape)),
    )
    halo = exchange(rim)
    sums = struct(*flat.shape, dtype=F32)
    pads_in, hidden, back_act = call(
        inner_kernel,
        (pads, sums, sums),
        (field, cot, weight_one, weight_two) + halo[:2],
        scratch,
        flags=False,
    )
    ends = pltpu.VMEM((3 * chans, 2 * LANES), BF16)
    shapes = (flat, flat, pads) + rim_shapes(chans)
    act, back, pads_in, *rim = pl.pallas_call(
        hidden_kernel,
        name="hidden",
        out_shape=shapes,
        in_specs=[SMEM, ANY] + [VMEM] * 6,
        out_specs=[VMEM, VMEM, ANY] + [VMEM] * (len(shapes) - 3),
        input_output_aliases={1: 2},
        scratch_shapes=[ends, ends, pltpu.SemaphoreType.DMA((2,))],
        compiler_params=pltpu.CompilerParams(vmem_limit_bytes=56 * 1024 * 1024),
    )(edge_flips, pads_in, hidden, back_act, weight_one, weight_two, *halo[2:])
    halo = exchange(rim)
    local = (struct(9 * chans, LANES, dtype=F32), struct(9 * chans, LANES))
    halves = [pltpu.VMEM((2, 9 * chans, LANES), F32)]
    one = call(grad_kernel, local, (back, pads_in), halves, flags=False)
    one = fold(one)
    pads_act, *two = call(grad_two_kernel, (pads,) + local, (edge_flips, act, cot) + halo, halves)
    two = fold(two)
    output = call(output_kernel, tile, (field, weight_two, pads_act), flags=False)
    quarter = reduce_grads(one, two)
    other = beside(quarter)
    grad_fields = call(
        grad_fields_kernel, tile, (edge_flips, cot, back, weight_one) + halo, scratch
    )
    pair = paired(quarter)
    across = paired(other)
    grads = finish(True, quarter, other)
    grad_one, grad_two = finish(False, pair, across, *grads)
    return (output.reshape(fields.shape), grad_fields.reshape(fields.shape), grad_one, grad_two)


def solution(mesh):
    in_specs = (P("dp", None, "lat", "lon"), P(), P(), P(), P("dp", None, "lat", "lon"))
    out_specs = (P("dp", None, "lat", "lon"), P("dp", None, "lat", "lon"), P(), P())


    return jax.shard_map(
        per_device, mesh=mesh, in_specs=in_specs, out_specs=out_specs, check_vma=False
    )
```
